32 devices in a mesh: seq: 8 (over z, x), tok: 4 (over y, core).
Axes of the slice: x: 2, y: 2, z: 4, core: 2. Of those that a mesh axis runs over, the one named last changes fastest.
Arguments:
- inputs: bfloat16 [16, 1536, 768], P('seq', 'tok'), may hold values from -6 to 6
- lengths: int32 [16], P('seq'), may hold values from 1024 to 1500, as said below
- matrices: float32 [7077888], P(('seq', 'tok')), may hold values from -2 to 2
- vectors: float32 [9216], P(('seq', 'tok')), may hold values from -2 to 2
- cotangent: bfloat16 [16, 1536, 768], P('seq', 'tok'), may hold values from -6 to 6
Outputs:
- outputs: bfloat16 [16, 1536, 768], P('seq', 'tok')
- grad_inputs: bfloat16 [16, 1536, 768], P('seq', 'tok')
- grad_matrices: float32 [7077888], P(('seq', 'tok'))
- grad_vectors: float32 [9216], P(('seq', 'tok'))
The draws below stay inside these ranges and needn't reach their ends.
Inputs may be any that keep to these rules, and one draw needn't show every extreme that they name: `lengths`: the valid slots of a sequence are its first ones; both ends of the range occur in every draw.
All inputs are finite; a program needn't handle non-finite values.
Results may differ from the reference program's by a relative error of at most 0.015.
The reference program's roundings to bfloat16 on the way count: a program that leaves them out, or rounds other values in their place, can miss the bound.
Values may be sent and summed in bfloat16 or wider, within the bound.
A program may use at most 192 MiB of HBM per device.

```python
import math
import jax
import jax.numpy as jnp
from jax import lax

D = 768
HEADS = 12
HEAD = 64
FF = 3072
SLOTS = 1536
SEQS = 16


def draw_lengths(key, part):
    lowest = SLOTS * 2 // 3
    highest = SLOTS * 125 // 128
    sample = jax.random.randint(key, (SEQS,), lowest, highest + 1)
    places = jax.random.permutation(jax.random.fold_in(key, 7), SEQS)
    positions = jnp.arange(SEQS)
    sample = jnp.where(positions == places[0], highest, sample)
    sample = jnp.where(positions == places[1], lowest, sample)
    return sample.astype(jnp.int32)


def draw_matrices(key, part):
    square = D * D
    entries = 4 * square + 2 * D * FF
    places = jnp.arange(entries)
    factor = jnp.where(places < square, 2.0 / math.sqrt(D), 1.0 / math.sqrt(D))
    factor = jnp.where((places >= 3 * square) & (places < 4 * square), 4.0 / math.sqrt(D), factor)
    factor = jnp.where(places >= 4 * square + D * FF, 2.0 / math.sqrt(FF), factor)
    sample = jax.random.normal(key, (entries,), jnp.float32)
    return (sample * factor).astype(jnp.float32)


def draw_vectors(key, part):
    entries = 8 * D + FF
    places = jnp.arange(entries)
    gain_part = (places < D) | (places >= 5 * D) & (places < 6 * D)
    sample = jax.random.normal(key, (entries,), jnp.float32)
    gains = jax.random.uniform(jax.random.fold_in(key, 3), (entries,), jnp.float32, 0.6, 1.4)
    return jnp.where(gain_part, gains, 0.3 * sample).astype(jnp.float32)


def shard_levels(own_key, shape, cuts, least, high):
    def one(dim, blocks):
        draws = jax.random.uniform(jax.random.fold_in(jax.random.fold_in(own_key, 6), dim), (blocks,), jnp.float32, least / len(cuts), high / len(cuts))
        return jnp.repeat(jnp.exp(draws), shape[dim] // blocks).reshape((-1,) + (1,) * (len(shape) - dim - 1))

    loudness = one(*cuts[0])
    for cut in cuts[1:]:
        loudness = loudness * one(*cut)
    return loudness


def normal_values(rng, shape, scale, most, split=(), kind=jnp.bfloat16):
    level = shard_levels(rng, shape, split, -0.22, 0.18) if split else 1.0
    result = jax.random.normal(rng, shape, jnp.float32) * scale * level
    return jnp.minimum(jnp.maximum(result, -most), most).astype(kind)


def setup_inputs(seed: int = 0) -> dict:
    key_of = jax.random.split(jax.random.key(seed), 6)
    return {
        "inputs": normal_values(key_of[0], (SEQS, SLOTS, D), 1.0, 6.0, ((0, 8), (1, 4))),
        "lengths": draw_lengths(jax.random.fold_in(key_of[5], 71), 0),
        "matrices": draw_matrices(jax.random.fold_in(key_of[5], 71), 0),
        "vectors": draw_vectors(jax.random.fold_in(key_of[5], 71), 0),
        "cotangent": normal_values(key_of[4], (SEQS, SLOTS, D), 1.0, 6.0, ((0, 8), (1, 4))),
    }


@jax.custom_vjp
def low(v):
    return lax.optimization_barrier(v.astype(jnp.bfloat16)).astype(jnp.float32)

@jax.custom_vjp
def low_back(v):
    return v

def low_keep(v):
    return (low(v), None)

def low_pass(kept, grad):
    return (grad,)

def back_keep(v):
    return (v, None)

def back_low(kept, grad):
    return (low(grad),)
low.defvjp(low_keep, low_pass)
low_back.defvjp(back_keep, back_low)
finest_precision = lax.Precision.HIGHEST

def both_round(value):
    return low(low_back(value))

def layer_norm(token_rows, norm_gain, norm_shift):
    center = lax.optimization_barrier(jnp.mean(token_rows, axis=-1, keepdims=True))
    centered = token_rows - center
    spread = lax.optimization_barrier(jnp.mean(centered * centered, axis=-1, keepdims=True))
    return centered * lax.rsqrt(spread + 1e-05) * norm_gain + norm_shift

def split_matrices(flattened):
    square = D * D
    rectangle = D * FF
    w_query = flattened[0:square].reshape(D, D)
    w_key = flattened[square:2 * square].reshape(D, D)
    w_value = flattened[2 * square:3 * square].reshape(D, D)
    w_out = flattened[3 * square:4 * square].reshape(D, D)
    w_up = flattened[4 * square:4 * square + rectangle].reshape(D, FF)
    w_down = flattened[4 * square + rectangle:4 * square + 2 * rectangle].reshape(FF, D)
    return (w_query, w_key, w_value, w_out, w_up, w_down)

def split_vectors(flattened):
    pieces = []
    for number in range(7):
        pieces.append(flattened[number * D:(number + 1) * D])
    pieces.append(flattened[7 * D:7 * D + FF])
    pieces.append(flattened[7 * D + FF:8 * D + FF])
    return tuple(pieces)

def project(left_operand, right_operand):
    return jnp.einsum('fnc,cj->fnj', left_operand, right_operand, precision=finest_precision)

def attend_sequence(pieces):
    query, key_rows, value_rows, length = pieces
    head_query = query.reshape(-1, HEADS, HEAD)
    head_keys = key_rows.reshape(-1, HEADS, HEAD)
    head_values = value_rows.reshape(-1, HEADS, HEAD)
    scores = jnp.einsum('qhd,khd->hqk', head_query, head_keys, precision=finest_precision) * HEAD ** (-0.5)
    valid = jnp.arange(SLOTS) < length
    scores = low_back(jnp.where(valid[None, None, :], scores, -1e+30))
    soft = low(jax.nn.softmax(scores, axis=-1))
    attended = jnp.einsum('hqk,khd->qhd', soft, head_values, precision=finest_precision)
    return attended.reshape(-1, D)

def forward(inputs, matrices, vectors, lengths):
    w_query, w_key, w_value, w_out, w_up, w_down = split_matrices(low(matrices))
    gain_one, first_norm_shift, bias_query, bias_value, bias_out, gain_two, shift_two, bias_up, bias_down = split_vectors(low(vectors))
    normed = low(layer_norm(inputs, gain_one, first_norm_shift))
    query = both_round(project(normed, w_query) + bias_query)
    key_rows = both_round(project(normed, w_key))
    value_rows = both_round(project(normed, w_value) + bias_value)
    attended = lax.map(jax.checkpoint(attend_sequence), (query, key_rows, value_rows, lengths))
    attended = both_round(attended)
    middle = inputs + low_back(project(attended, w_out) + bias_out)
    normed_two = low(layer_norm(middle, gain_two, shift_two))
    hidden = low_back(project(normed_two, w_up) + bias_up)
    active = low(jax.nn.gelu(hidden, approximate=False))
    return middle + low_back(project(active, w_down) + bias_down)

def reference(inputs, lengths, matrices, vectors, cotangent):

    def wrapped(frames, flat_mats, flat_vecs):
        return forward(frames, flat_mats, flat_vecs, lengths)
    outputs, pullback = jax.vjp(wrapped, inputs.astype(jnp.float32), matrices, vectors)
    grad_inputs, grad_matrices, grad_vectors = pullback(cotangent.astype(jnp.float32))
    return (outputs.astype(jnp.bfloat16), grad_inputs.astype(jnp.bfloat16), grad_matrices, grad_vectors)
```

```python
from functools import partial

import jax
import jax.numpy as jnp
from jax import lax
from jax.experimental import pallas as pl
from jax.experimental.pallas import tpu as pltpu
from jax.sharding import PartitionSpec as P

D = 768
HEADS = 12
HEAD = 64
FF = 3072
PAIRS = HEADS // 2
LANES = 2 * HEAD
F32 = jnp.float32
BF16 = jnp.bfloat16
VMEM_LIMIT = 56 * 1024 * 1024


def layer_norm(token_rows, norm_gain, norm_shift):
    center = jnp.mean(token_rows, axis=-1, keepdims=True)
    centered = token_rows - center
    spread = jnp.mean(centered * centered, axis=-1, keepdims=True)
    return centered * lax.rsqrt(spread + 1e-05) * norm_gain + norm_shift


def matmul(left_operand, right_operand):
    return jnp.dot(left_operand, right_operand, preferred_element_type=F32)


def outer_sum(left_operand, right_operand):
    return lax.dot_general(
        left_operand, right_operand, (((0,), (0,)), ((), ())), preferred_element_type=F32
    )


def back_product(gradient, weight):
    return lax.dot_general(
        gradient, weight, (((1,), (1,)), ((), ())), preferred_element_type=F32
    )


def column_sum(gradient):
    return jnp.sum(gradient.astype(F32), axis=0)


def pair_columns(pair):
    return pl.ds(pl.multiple_of(pair * LANES, LANES), LANES)


def forward_pair(pair, q_ref, k_ref, v_ref, bias_ref, o_ref, l_ref, row_chunk):
    rows = q_ref.shape[0]
    keys = k_ref.shape[0]
    cols = pair_columns(pair)
    lane_k = lax.broadcasted_iota(jnp.int32, (keys, LANES), 1)
    lane_q = lax.broadcasted_iota(jnp.int32, (row_chunk, LANES), 1)
    lane_l = lax.broadcasted_iota(jnp.int32, (row_chunk, LANES), 1)
    key_pair = k_ref[:, cols]
    value_pair = v_ref[:, cols]
    bias = bias_ref[...]
    head_keys = []
    for half in range(2):
        own = lane_k // HEAD == half
        spare = lane_k == (1 - half) * HEAD
        head_keys.append(jnp.where(own, key_pair, jnp.where(spare, bias, jnp.zeros_like(bias))))
    for chunk in range(rows // row_chunk):
        part = pl.ds(chunk * row_chunk, row_chunk)
        query_pair = q_ref[part, cols]
        one = jnp.ones_like(query_pair)
        results = []
        masses = l_ref[part, :]
        for half in range(2):
            own_q = lane_q // HEAD == half
            query = jnp.where(own_q, query_pair, one)
            scores = lax.dot_general(
                query, head_keys[half], (((1,), (1,)), ((), ())), preferred_element_type=F32
            )
            peak = jnp.max(scores, axis=-1, keepdims=True)
            raised = jnp.exp(scores - peak)
            mass = jnp.sum(raised, axis=-1, keepdims=True)
            soft = (raised * (1.0 / mass)).astype(BF16)
            results.append(matmul(soft, value_pair))
            masses = jnp.where(lane_l == 2 * pair + half, peak + jnp.log(mass), masses)
        l_ref[part, :] = masses
        o_ref[part, cols] = jnp.where(lane_q // HEAD == 0, results[0], results[1]).astype(BF16)


def forward_kernel(row_chunk, q_ref, k_ref, v_ref, bias_ref, o_ref, lt_ref, l_ref):
    l_ref[...] = jnp.zeros_like(l_ref)

    def step(pair, carry):
        forward_pair(pair, q_ref, k_ref, v_ref, bias_ref, o_ref, l_ref, row_chunk)
        return carry

    lax.fori_loop(0, PAIRS, step, 0)
    lt_ref[...] = l_ref[...].T[: lt_ref.shape[0]]


def attend(query, keys, values, bias):
    rows = query.shape[0]
    vmem = pl.BlockSpec(memory_space=pltpu.VMEM)
    return pl.pallas_call(
        partial(forward_kernel, 256),
        out_shape=(
            jax.ShapeDtypeStruct((rows, D), BF16),
            jax.ShapeDtypeStruct((16, rows), F32),
        ),
        in_specs=[vmem] * 4,
        out_specs=(vmem, vmem),
        scratch_shapes=[pltpu.VMEM((rows, LANES), F32)],
        compiler_params=pltpu.CompilerParams(vmem_limit_bytes=VMEM_LIMIT),
        name="attend",
    )(query, keys, values, bias)


def backward_pair(
    pair, q_ref, k_ref, v_ref, bias_ref, g_ref, lt_ref, dt_ref, dq_ref, dk_ref, dv_ref, key_chunk
):
    rows = q_ref.shape[0]
    keys = k_ref.shape[0]
    cols = pair_columns(pair)
    lane_k = lax.broadcasted_iota(jnp.int32, (key_chunk, LANES), 1)
    lane_q = lax.broadcasted_iota(jnp.int32, (rows, LANES), 1)
    query_pair = q_ref[:, cols]
    grad_pair = g_ref[:, cols]
    one = jnp.ones_like(query_pair)
    query_heads = [jnp.where(lane_q // HEAD == half, query_pair, one) for half in range(2)]
    zero = jnp.zeros((key_chunk, LANES), BF16)
    grad_query = [jnp.zeros((rows, LANES), F32) for _ in range(2)]
    for chunk in range(keys // key_chunk):
        part = pl.ds(chunk * key_chunk, key_chunk)
        key_pair = k_ref[part, cols]
        value_pair = v_ref[part, cols]
        bias = bias_ref[part, :]
        grad_key = []
        grad_value = []
        for half in range(2):
            own = lane_k // HEAD == half
            spare = lane_k == (1 - half) * HEAD
            head_key = jnp.where(own, key_pair, jnp.where(spare, bias, jnp.zeros_like(bias)))
            head_value = jnp.where(own, value_pair, zero)
            scores = back_product(head_key, query_heads[half])
            mass = lt_ref[pl.ds(2 * pair + half, 1), :]
            inner = dt_ref[pl.ds(2 * pair + half, 1), :]
            soft = jnp.exp(scores - mass)
            grad_soft = back_product(head_value, grad_pair)
            grad_scores = (soft * (grad_soft - inner)).astype(BF16)
            grad_value.append(matmul(soft.astype(BF16), grad_pair))
            grad_key.append(matmul(grad_scores, query_pair))
            grad_query[half] = grad_query[half] + outer_sum(grad_scores, key_pair)
        first = lane_k // HEAD == 0
        dk_ref[part, cols] = jnp.where(first, grad_key[0], grad_key[1]).astype(BF16)
        dv_ref[part, cols] = jnp.where(first, grad_value[0], grad_value[1]).astype(BF16)
    merged = jnp.where(lane_q // HEAD == 0, grad_query[0], grad_query[1])
    dq_ref[:, cols] = (merged * HEAD ** (-0.5)).astype(BF16)


def backward_kernel(key_chunk, *refs):
    def step(pair, carry):
        backward_pair(pair, *refs, key_chunk)
        return carry

    lax.fori_loop(0, PAIRS, step, 0)


def attend_back(query, keys, values, bias, grad, lt, dt):
    vmem = pl.BlockSpec(memory_space=pltpu.VMEM)
    return pl.pallas_call(
        partial(backward_kernel, 256),
        out_shape=(
            jax.ShapeDtypeStruct(query.shape, BF16),
            jax.ShapeDtypeStruct(keys.shape, BF16),
            jax.ShapeDtypeStruct(keys.shape, BF16),
        ),
        in_specs=[vmem] * 7,
        out_specs=(vmem,) * 3,
        compiler_params=pltpu.CompilerParams(vmem_limit_bytes=VMEM_LIMIT),
        name="attend_back",
    )(query, keys, values, bias, grad, lt, dt)


def split_matrices(rows):
    w_up = rows[4 * D : 4 * D + FF].reshape(D, FF)
    w_down = rows[4 * D + FF : 4 * D + 2 * FF]
    return (rows[:D], rows[D : 2 * D], rows[2 * D : 3 * D], rows[3 * D : 4 * D], w_up, w_down)


def split_vectors(flattened):
    pieces = []
    for number in range(7):
        pieces.append(flattened[number * D : (number + 1) * D])
    pieces.append(flattened[7 * D : 7 * D + FF])
    pieces.append(flattened[7 * D + FF : 8 * D + FF])
    return tuple(pieces)


def local(inputs, lengths, matrices, vectors, cotangent):
    seq_count, local_slots, width = inputs.shape
    tok_size = lax.axis_size("tok")
    tok = lax.axis_index("tok")
    half = tok // 2
    devices = tok_size * lax.axis_size("seq")
    rows = seq_count * local_slots
    across = [(i, (i + 2) % 4) for i in range(4)]
    partner = [(i, i + 1 - 2 * (i % 2)) for i in range(4)]

    def pick(array, index):
        return lax.dynamic_index_in_dim(array, index, 0, keepdims=False)

    def to_sequence(array):
        other = lax.ppermute(pick(array, 1 - half), "tok", across)
        return jnp.concatenate([pick(array, half), other], axis=0)

    def from_sequence(array):
        other = lax.ppermute(array[local_slots:], "tok", across)
        kept = array[:local_slots]
        return jnp.where(half == 0, jnp.stack([kept, other]), jnp.stack([other, kept]))

    shard_rows = matrices.shape[0] // width
    low_rows = matrices.reshape(shard_rows, width).astype(BF16)
    gathered = lax.all_gather(low_rows, ("seq", "tok"), axis=0, tiled=True)
    w_query, w_key, w_value, w_out, w_up, w_down = split_matrices(gathered)
    vec_count = vectors.shape[0]
    vec_rows = 8
    vec_pad = vec_rows * 128 - vec_count
    vec_low = jnp.pad(vectors, (0, vec_pad)).astype(BF16).reshape(vec_rows, 128)
    vecs = lax.all_gather(vec_low, ("seq", "tok"), axis=0, tiled=True)
    vecs = vecs.reshape(devices, vec_rows * 128)[:, :vec_count].reshape(-1)
    (
        gain_one,
        first_norm_shift,
        bias_query,
        bias_value,
        bias_out,
        gain_two,
        shift_two,
        bias_up,
        bias_down,
    ) = split_vectors(vecs.astype(F32))

    token_rows = to_sequence(inputs).astype(F32)
    grad_out = to_sequence(cotangent)
    length = pick(lengths, half)
    slot = jnp.arange(local_slots, dtype=jnp.int32)
    places = jnp.concatenate([block * local_slots + slot for block in (tok, tok ^ 2, tok ^ 1, tok ^ 3)])
    bias = jnp.where(places < length, 0.0, -1e30).astype(BF16)[:, None]
    bias = jnp.broadcast_to(bias, (bias.shape[0], LANES))

    normed = layer_norm(token_rows, gain_one, first_norm_shift).astype(BF16)
    query = (matmul(normed, w_query) + bias_query).astype(BF16)
    scaled = query * jnp.asarray(HEAD ** (-0.5), BF16)
    keys_here = matmul(normed, w_key).astype(BF16)
    values_here = (matmul(normed, w_value) + bias_value).astype(BF16)
    keys = jnp.concatenate([keys_here, lax.ppermute(keys_here, "tok", partner)], axis=0)
    values = jnp.concatenate([values_here, lax.ppermute(values_here, "tok", partner)], axis=0)
    attended, lt = attend(scaled, keys, values, bias)
    middle = token_rows + (matmul(attended, w_out) + bias_out)
    normed_two = layer_norm(middle, gain_two, shift_two).astype(BF16)
    hidden = matmul(normed_two, w_up) + bias_up
    active = jax.nn.gelu(hidden, approximate=False).astype(BF16)
    result = middle + (matmul(active, w_down) + bias_down)
    outputs = from_sequence(result.astype(BF16))

    grad_out_wide = grad_out.astype(F32)
    d_down = outer_sum(active, grad_out)
    down_bias_gradient = column_sum(grad_out)
    grad_active = back_product(grad_out, w_down)
    gelu_value, gelu_pull = jax.vjp(partial(jax.nn.gelu, approximate=False), hidden)
    grad_hidden = gelu_pull(grad_active)[0].astype(BF16)
    d_up = outer_sum(normed_two, grad_hidden)
    d_bias_up = column_sum(grad_hidden)
    grad_normed_two = back_product(grad_hidden, w_up)
    norm_value, norm_pull = jax.vjp(layer_norm, middle, gain_two, shift_two)
    grad_mid_norm, d_gain_two, d_shift_two = norm_pull(grad_normed_two)
    grad_middle = grad_out_wide + grad_mid_norm
    grad_branch = grad_middle.astype(BF16)
    d_out = outer_sum(attended, grad_branch)
    d_bias_out = column_sum(grad_branch)
    grad_attended = back_product(grad_branch, w_out).astype(BF16)
    inner = (grad_attended.astype(F32) * attended.astype(F32)).reshape(rows, HEADS, HEAD).sum(-1)
    inner = jnp.pad(inner.T, ((0, 16 - HEADS), (0, 0)))
    grad_query, grad_keys, grad_values = attend_back(
        scaled, keys, values, bias, grad_attended, lt, inner
    )

    def pair_sum(array):
        other = lax.ppermute(array[rows:], "tok", partner)
        return (array[:rows].astype(F32) + other.astype(F32)).astype(BF16)

    grad_key = pair_sum(grad_keys)
    grad_value = pair_sum(grad_values)
    d_query = outer_sum(normed, grad_query)
    d_key = outer_sum(normed, grad_key)
    d_value = outer_sum(normed, grad_value)
    d_bias_query = column_sum(grad_query)
    d_bias_value = column_sum(grad_value)
    grad_normed = (
        back_product(grad_query, w_query)
        + back_product(grad_key, w_key)
        + back_product(grad_value, w_value)
    )
    first_value, leading_pullback = jax.vjp(layer_norm, token_rows, gain_one, first_norm_shift)
    grad_rows_norm, d_gain_one, d_shift_one = leading_pullback(grad_normed)
    grad_inputs = from_sequence((grad_middle + grad_rows_norm).astype(BF16))
    matrix_rows = jnp.concatenate(
        [
            piece.astype(BF16).reshape(-1, width)
            for piece in (d_query, d_key, d_value, d_out, d_up, d_down)
        ]
    )
    flat_vector_grads = jnp.concatenate(
        [
            d_gain_one,
            d_shift_one,
            d_bias_query,
            d_bias_value,
            d_bias_out,
            d_gain_two,
            d_shift_two,
            d_bias_up,
            down_bias_gradient,
        ]
    )
    vector_rows = jnp.pad(flat_vector_grads.reshape(devices, vec_count), ((0, 0), (0, vec_pad)))
    grad_rows = lax.psum_scatter(
        matrix_rows, ("seq", "tok"), scatter_dimension=0, tiled=True
    )
    grad_vec_rows = lax.psum_scatter(
        vector_rows.reshape(devices * vec_rows, 128), ("seq", "tok"), scatter_dimension=0, tiled=True
    )
    grad_matrices = grad_rows.astype(F32).reshape(-1)
    grad_vectors = grad_vec_rows.reshape(-1)[:vec_count]
    return (outputs, grad_inputs, grad_matrices, grad_vectors)


def solution(mesh):
    in_specs = (
        P("seq", "tok", None),
        P("seq"),
        P(("seq", "tok")),
        P(("seq", "tok")),
        P("seq", "tok", None),
    )
    out_specs = (P("seq", "tok", None), P("seq", "tok", None), P(("seq", "tok")), P(("seq", "tok")))
    return jax.shard_map(local, mesh=mesh, in_specs=in_specs, out_specs=out_specs, check_vma=False)
```

```python
from functools import partial

import jax
import jax.numpy as jnp
from jax import lax
from jax.experimental import pallas as pl
from jax.experimental.pallas import tpu as pltpu
from jax.sharding import PartitionSpec as P

D = 768
HEADS = 12
HEAD = 64
FF = 3072
PAIRS = HEADS // 2
LANES = 2 * HEAD
F32 = jnp.float32
BF16 = jnp.bfloat16
VMEM_LIMIT = 56 * 1024 * 1024


def layer_norm(token_rows, norm_gain, norm_shift):
    center = jnp.mean(token_rows, axis=-1, keepdims=True)
    centered = token_rows - center
    spread = jnp.mean(centered * centered, axis=-1, keepdims=True)
    return centered * lax.rsqrt(spread + 1e-05) * norm_gain + norm_shift


def matmul(left_operand, right_operand):
    return jnp.dot(left_operand, right_operand, preferred_element_type=F32)


def outer_sum(left_operand, right_operand):
    return lax.dot_general(
        left_operand, right_operand, (((0,), (0,)), ((), ())), preferred_element_type=F32
    )


def back_product(gradient, weight):
    return lax.dot_general(
        gradient, weight, (((1,), (1,)), ((), ())), preferred_element_type=F32
    )


def column_sum(gradient):
    return jnp.sum(gradient.astype(F32), axis=0)


def pair_columns(pair):
    return pl.ds(pl.multiple_of(pair * LANES, LANES), LANES)


def forward_pair(pair, q_ref, k_ref, v_ref, bias_ref, o_ref, l_ref, row_chunk):
    rows = q_ref.shape[0]
    keys = k_ref.shape[0]
    cols = pair_columns(pair)
    lane_k = lax.broadcasted_iota(jnp.int32, (keys, LANES), 1)
    lane_q = lax.broadcasted_iota(jnp.int32, (row_chunk, LANES), 1)
    lane_l = lax.broadcasted_iota(jnp.int32, (row_chunk, LANES), 1)
    key_pair = k_ref[:, cols]
    value_pair = v_ref[:, cols]
    bias = bias_ref[...]
    head_keys = []
    for half in range(2):
        own = lane_k // HEAD == half
        spare = lane_k == (1 - half) * HEAD
        head_keys.append(jnp.where(own, key_pair, jnp.where(spare, bias, jnp.zeros_like(bias))))
    for chunk in range(rows // row_chunk):
        part = pl.ds(chunk * row_chunk, row_chunk)
        query_pair = q_ref[part, cols]
        one = jnp.ones_like(query_pair)
        results = []
        masses = l_ref[part, :]
        for half in range(2):
            own_q = lane_q // HEAD == half
            query = jnp.where(own_q, query_pair, one)
            scores = lax.dot_general(
                query, head_keys[half], (((1,), (1,)), ((), ())), preferred_element_type=F32
            )
            peak = jnp.max(scores, axis=-1, keepdims=True)
            raised = jnp.exp(scores - peak)
            mass = jnp.sum(raised, axis=-1, keepdims=True)
            soft = (raised * (1.0 / mass)).astype(BF16)
            results.append(matmul(soft, value_pair))
            masses = jnp.where(lane_l == 2 * pair + half, peak + jnp.log(mass), masses)
        l_ref[part, :] = masses
        o_ref[part, cols] = jnp.where(lane_q // HEAD == 0, results[0], results[1]).astype(BF16)


def forward_kernel(row_chunk, q_ref, k_ref, v_ref, bias_ref, o_ref, lt_ref, l_ref):
    l_ref[...] = jnp.zeros_like(l_ref)

    def step(pair, carry):
        forward_pair(pair, q_ref, k_ref, v_ref, bias_ref, o_ref, l_ref, row_chunk)
        return carry

    lax.fori_loop(0, PAIRS, step, 0)
    lt_ref[...] = l_ref[...].T[: lt_ref.shape[0]]


def attend(query, keys, values, bias):
    rows = query.shape[0]
    vmem = pl.BlockSpec(memory_space=pltpu.VMEM)
    return pl.pallas_call(
        partial(forward_kernel, 256),
        out_shape=(
            jax.ShapeDtypeStruct((rows, D), BF16),
            jax.ShapeDtypeStruct((16, rows), F32),
        ),
        in_specs=[vmem] * 4,
        out_specs=(vmem, vmem),
        scratch_shapes=[pltpu.VMEM((rows, LANES), F32)],
        compiler_params=pltpu.CompilerParams(vmem_limit_bytes=VMEM_LIMIT),
        name="attend",
    )(query, keys, values, bias)


def backward_pair(
    pair, q_ref, k_ref, v_ref, bias_ref, g_ref, lt_ref, dt_ref, dq_ref, dk_ref, dv_ref, key_chunk
):
    rows = q_ref.shape[0]
    keys = k_ref.shape[0]
    cols = pair_columns(pair)
    lane_k = lax.broadcasted_iota(jnp.int32, (key_chunk, LANES), 1)
    lane_q = lax.broadcasted_iota(jnp.int32, (rows, LANES), 1)
    query_pair = q_ref[:, cols]
    grad_pair = g_ref[:, cols]
    one = jnp.ones_like(query_pair)
    query_heads = [jnp.where(lane_q // HEAD == half, query_pair, one) for half in range(2)]
    zero = jnp.zeros((key_chunk, LANES), BF16)
    grad_query = [jnp.zeros((rows, LANES), F32) for _ in range(2)]
    for chunk in range(keys // key_chunk):
        part = pl.ds(chunk * key_chunk, key_chunk)
        key_pair = k_ref[part, cols]
        value_pair = v_ref[part, cols]
        bias = bias_ref[part, :]
        grad_key = []
        grad_value = []
        for half in range(2):
            own = lane_k // HEAD == half
            spare = lane_k == (1 - half) * HEAD
            head_key = jnp.where(own, key_pair, jnp.where(spare, bias, jnp.zeros_like(bias)))
            head_value = jnp.where(own, value_pair, zero)
            scores = back_product(head_key, query_heads[half])
            mass = lt_ref[pl.ds(2 * pair + half, 1), :]
            inner = dt_ref[pl.ds(2 * pair + half, 1), :]
            soft = jnp.exp(scores - mass)
            grad_soft = back_product(head_value, grad_pair)
            grad_scores = (soft * (grad_soft - inner)).astype(BF16)
            grad_value.append(matmul(soft.astype(BF16), grad_pair))
            grad_key.append(matmul(grad_scores, query_pair))
            grad_query[half] = grad_query[half] + outer_sum(grad_scores, key_pair)
        first = lane_k // HEAD == 0
        dk_ref[part, cols] = jnp.where(first, grad_key[0], grad_key[1]).astype(BF16)
        dv_ref[part, cols] = jnp.where(first, grad_value[0], grad_value[1]).astype(BF16)
    merged = jnp.where(lane_q // HEAD == 0, grad_query[0], grad_query[1])
    dq_ref[:, cols] = (merged * HEAD ** (-0.5)).astype(BF16)


def backward_kernel(key_chunk, *refs):
    def step(pair, carry):
        backward_pair(pair, *refs, key_chunk)
        return carry

    lax.fori_loop(0, PAIRS, step, 0)


def attend_back(query, keys, values, bias, grad, lt, dt):
    vmem = pl.BlockSpec(memory_space=pltpu.VMEM)
    return pl.pallas_call(
        partial(backward_kernel, 256),
        out_shape=(
            jax.ShapeDtypeStruct(query.shape, BF16),
            jax.ShapeDtypeStruct(keys.shape, BF16),
            jax.ShapeDtypeStruct(keys.shape, BF16),
        ),
        in_specs=[vmem] * 7,
        out_specs=(vmem,) * 3,
        compiler_params=pltpu.CompilerParams(vmem_limit_bytes=VMEM_LIMIT),
        name="attend_back",
    )(query, keys, values, bias, grad, lt, dt)


def split_matrices(rows):
    w_up = rows[4 * D : 4 * D + FF].reshape(D, FF)
    w_down = rows[4 * D + FF : 4 * D + 2 * FF]
    return (rows[:D], rows[D : 2 * D], rows[2 * D : 3 * D], rows[3 * D : 4 * D], w_up, w_down)


def split_vectors(flattened):
    pieces = []
    for number in range(7):
        pieces.append(flattened[number * D : (number + 1) * D])
    pieces.append(flattened[7 * D : 7 * D + FF])
    pieces.append(flattened[7 * D + FF : 8 * D + FF])
    return tuple(pieces)


SHARD = 288
CHUNKS = 3
CHUNK = SHARD // CHUNKS
MESH = pl.DeviceIdType.MESH
UP, DOWN, NEAR_X, NEAR_Y, DIAG_A, DIAG_B, PAIR_C, PAIR_X, PAIR_Y, PAIR_A, PAIR_B = range(11)


class Place:
    def __init__(self):
        self.seq = lax.axis_index("seq")
        self.tok = lax.axis_index("tok")
        self.z = self.seq // 2
        self.x = self.seq % 2
        self.y = self.tok // 2
        self.c = self.tok % 2
        self.levels = lax.axis_size("seq") // 2
        self.up = (self.seq + 2, self.tok)
        self.down = (self.seq - 2, self.tok)
        self.near_x = (self.seq + 1 - 2 * self.x, self.tok)
        self.near_y = (self.seq, self.tok + 2 - 4 * self.y)
        self.pair = (self.seq, self.tok + 1 - 2 * self.c)
        self.has_up = self.z < self.levels - 1
        self.has_down = self.z > 0

    def barrier(self):
        sem = pltpu.get_barrier_semaphore()
        for device in (self.near_x, self.near_y, self.pair):
            pl.semaphore_signal(sem, inc=1, device_id=device, device_id_type=MESH)

        @pl.when(self.has_up)
        def _():
            pl.semaphore_signal(sem, inc=1, device_id=self.up, device_id_type=MESH)

        @pl.when(self.has_down)
        def _():
            pl.semaphore_signal(sem, inc=1, device_id=self.down, device_id_type=MESH)

        count = 3 + self.has_up.astype(jnp.int32) + self.has_down.astype(jnp.int32)
        pl.semaphore_wait(sem, count)


def remote(source, target, send, recv, device):
    return pltpu.make_async_remote_copy(
        src_ref=source,
        dst_ref=target,
        send_sem=send,
        recv_sem=recv,
        device_id=device,
        device_id_type=MESH,
    )


class Gather:
    def __init__(self, at, w_ref, send, recv, low, high, split):
        self.at, self.w, self.send, self.recv = at, w_ref, send, recv
        self.low, self.high, self.split = low, high, split
        self.steps = at.levels * CHUNKS + 2

    def piece(self, level, x, y, c, first, count):
        first = pl.multiple_of(first, 16)
        return self.w.at[level - self.low, x, y, c, pl.ds(first, count)]

    def copies(self, level, chunk):
        at, split = self.at, self.split
        x, y, c = at.x, at.y, at.c
        first = chunk * CHUNK

        def view(xs, ys, cs, low=0, count=CHUNK):
            return self.piece(level, xs, ys, cs, first + low, count)

        rest = CHUNK - split
        table = {
            UP: (view(x, y, c), view(x, y, c), at.up),
            DOWN: (view(x, y, c), view(x, y, c), at.down),
            NEAR_X: (view(x, y, c), view(1 - x, y, c), at.near_x),
            NEAR_Y: (view(x, y, c), view(x, 1 - y, c), at.near_y),
            PAIR_C: (view(x, y, c), view(x, y, 1 - c), at.pair),
            PAIR_X: (view(1 - x, y, c), view(1 - x, y, 1 - c), at.pair),
            PAIR_Y: (view(x, 1 - y, c), view(x, 1 - y, 1 - c), at.pair),
        }
        if split:
            table[DIAG_A] = (
                view(1 - x, y, c, 0, split),
                view(1 - x, 1 - y, c, 0, split),
                at.near_y,
            )
            table[PAIR_A] = (
                view(1 - x, 1 - y, c, 0, split),
                view(1 - x, 1 - y, 1 - c, 0, split),
                at.pair,
            )
        if rest:
            table[DIAG_B] = (
                view(x, 1 - y, c, split, rest),
                view(1 - x, 1 - y, c, split, rest),
                at.near_x,
            )
            table[PAIR_B] = (
                view(1 - x, 1 - y, c, split, rest),
                view(1 - x, 1 - y, 1 - c, split, rest),
                at.pair,
            )
        return table

    def start(self, table, kind, slot):
        sent, _, device = table[kind]
        remote(sent, sent, self.send.at[kind, slot], self.recv.at[kind, slot], device).start()

    def wait_recv(self, table, kind, slot):
        _, came, device = table[kind]
        remote(came, came, self.send.at[kind, slot], self.recv.at[kind, slot], device).wait_recv()

    def wait_send(self, table, kind, slot):
        sent, _, device = table[kind]
        remote(sent, sent, self.send.at[kind, slot], self.recv.at[kind, slot], device).wait_send()

    def items(self, index, body):
        at = self.at
        inside = (index >= 0) & (index < at.levels * CHUNKS)
        distance = jnp.where(inside, index // CHUNKS, 0)
        chunk = jnp.where(inside, index % CHUNKS, 0)
        for below in (True, False):
            level = at.z - distance if below else at.z + distance
            valid = inside & (level >= self.low) & (level <= self.high)
            if not below:
                valid = valid & (distance > 0)

            @pl.when(valid)
            def _(level=level, below=below):
                slot = level * CHUNKS + chunk
                body(slot, self.copies(level, chunk), distance == 0, below)

    def column(self, index):
        at = self.at

        def body(slot, table, own, below):
            @pl.when(jnp.logical_not(own))
            def _():
                self.wait_recv(table, UP if below else DOWN, slot)

            if below:

                @pl.when(at.has_up)
                def _():
                    self.start(table, UP, slot)

                @pl.when(own & at.has_down)
                def _():
                    self.start(table, DOWN, slot)

            else:

                @pl.when(at.has_down)
                def _():
                    self.start(table, DOWN, slot)

            for kind in (NEAR_Y, NEAR_X, PAIR_C):
                self.start(table, kind, slot)

        self.items(index, body)

    def plane(self, index):
        def body(slot, table, own, below):
            self.wait_recv(table, NEAR_Y, slot)
            for kind in (DIAG_B, PAIR_Y):
                if kind in table:
                    self.start(table, kind, slot)
            self.wait_recv(table, NEAR_X, slot)
            for kind in (DIAG_A, PAIR_X):
                if kind in table:
                    self.start(table, kind, slot)

        self.items(index, body)

    def diagonal(self, index):
        def body(slot, table, own, below):
            for kind, onward in ((DIAG_B, PAIR_B), (DIAG_A, PAIR_A)):
                if kind in table:
                    self.wait_recv(table, kind, slot)
                    self.start(table, onward, slot)

        self.items(index, body)

    def step(self, number):
        self.column(number)
        self.plane(number - 1)
        self.diagonal(number - 2)

    def finish(self):
        at = self.at

        def body(slot, table, own, below):
            for kind in (PAIR_C, PAIR_X, PAIR_Y, PAIR_A, PAIR_B):
                if kind in table:
                    self.wait_recv(table, kind, slot)
            if below:

                @pl.when(at.has_up)
                def _():
                    self.wait_send(table, UP, slot)

                @pl.when(own & at.has_down)
                def _():
                    self.wait_send(table, DOWN, slot)

            else:

                @pl.when(at.has_down)
                def _():
                    self.wait_send(table, DOWN, slot)

            for kind in table:
                if kind not in (UP, DOWN):
                    self.wait_send(table, kind, slot)

        def loop(index, carry):
            self.items(index, body)
            return carry

        lax.fori_loop(0, at.levels * CHUNKS, loop, 0)


class Scatter:
    def __init__(self, at, g_ref, out_ref, buffers, send, recv, local_sem, low, high):
        self.at, self.g, self.out, self.send, self.recv = at, g_ref, out_ref, send, recv
        self.acc, self.from_pair, self.x1, self.y1, self.x2, self.y2, self.za, self.zb = buffers
        self.local_sem, self.low, self.high = local_sem, low, high
        self.count = (high - low + 1) * CHUNKS
        self.last = at.levels + 2
        self.steps = self.count + self.last

    def half(self):
        return CHUNK // 2

    def views(self, item):
        at = self.at
        x, y, c = at.x, at.y, at.c
        index = item // CHUNKS
        first = pl.multiple_of((item % CHUNKS) * CHUNK, 16)
        h = self.half()
        rows = pl.ds(first, CHUNK)
        rows_a = pl.ds(first, h)
        rows_b = pl.ds(pl.multiple_of(first + h, 16), CHUNK - h)
        acc = self.acc
        mine = acc.at[index, x, y, rows]
        return {
            0: (self.g.at[index, :, :, 1 - c, rows], self.from_pair.at[index, :, :, rows], at.pair),
            1: (acc.at[index, 1 - x, :, rows_a], self.x1.at[item], at.near_x),
            2: (acc.at[index, :, 1 - y, rows_b], self.y1.at[item], at.near_y),
            3: (acc.at[index, x, 1 - y, rows_a], self.y2.at[item], at.near_y),
            4: (acc.at[index, 1 - x, y, rows_b], self.x2.at[item], at.near_x),
            5: (mine, self.zb.at[item], at.up),
            6: (mine, self.za.at[item], at.down),
        }, index, (rows, rows_a, rows_b)

    def copy(self, views, kind, item):
        source, target, device = views[kind]
        return remote(source, target, self.send.at[kind, item], self.recv.at[kind, item], device)

    def guarded(self, item, body, extra=None):
        valid = (item >= 0) & (item < self.count)
        item = jnp.where(valid, item, 0)
        level = self.low + item // CHUNKS
        if extra is not None:
            valid = valid & extra(level)

        @pl.when(valid)
        def _():
            views, index, rows = self.views(item)
            body(item, views, index, rows)

    def local(self, item, index, rows):
        return pltpu.make_async_copy(
            self.g.at[index, :, :, self.at.c, rows[0]],
            self.acc.at[index, :, :, rows[0]],
            self.local_sem.at[item],
        )

    def begin(self, item):
        def body(item, views, index, rows):
            self.copy(views, 0, item).start()
            self.local(item, index, rows).start()

        self.guarded(item, body)

    @staticmethod
    def add(target, where, addend):
        target[where] = (target[where].astype(F32) + addend.astype(F32)).astype(BF16)

    def first(self, item):
        def body(item, views, index, rows):
            self.copy(views, 0, item).wait_recv()
            self.local(item, index, rows).wait()
            for xs in range(2):
                for ys in range(2):
                    where = (index, xs, ys, rows[0])
                    self.add(self.acc, where, self.from_pair[where])
            self.copy(views, 1, item).start()
            self.copy(views, 2, item).start()

        self.guarded(item, body)

    def second(self, item):
        at = self.at

        def body(item, views, index, rows):
            self.copy(views, 1, item).wait_recv()
            for ys in range(2):
                self.add(self.acc, (index, at.x, ys, rows[1]), self.x1[item, ys])
            self.copy(views, 3, item).start()
            self.copy(views, 2, item).wait_recv()
            for xs in range(2):
                self.add(self.acc, (index, xs, at.y, rows[2]), self.y1[item, xs])
            self.copy(views, 4, item).start()

        self.guarded(item, body)

    def collect(self, item, views, index, rows):
        at = self.at
        self.copy(views, 3, item).wait_recv()
        self.copy(views, 4, item).wait_recv()
        self.add(self.acc, (index, at.x, at.y, rows[1]), self.y2[item])
        self.add(self.acc, (index, at.x, at.y, rows[2]), self.x2[item])

    def along(self, step):
        at = self.at

        def rise(item, views, index, rows):
            self.collect(item, views, index, rows)

            @pl.when(at.has_down)
            def _():
                self.copy(views, 5, item).wait_recv()
                self.add(self.acc, (index, at.x, at.y, rows[0]), self.zb[item])

            self.copy(views, 5, item).start()

        def sink(item, views, index, rows):
            self.collect(item, views, index, rows)

            @pl.when(at.has_up)
            def _():
                self.copy(views, 6, item).wait_recv()
                self.add(self.acc, (index, at.x, at.y, rows[0]), self.za[item])

            self.copy(views, 6, item).start()

        def arrive(item, views, index, rows):
            self.collect(item, views, index, rows)
            self.out[rows[0]] = self.acc[index, at.x, at.y, rows[0]].astype(F32)

            @pl.when(at.has_down)
            def _():
                self.copy(views, 5, item).wait_recv()
                self.out[rows[0]] = self.out[rows[0]] + self.zb[item].astype(F32)

            @pl.when(at.has_up)
            def _():
                self.copy(views, 6, item).wait_recv()
                self.out[rows[0]] = self.out[rows[0]] + self.za[item].astype(F32)

        top = at.levels - 1
        self.guarded(step - 3 - at.z, rise, lambda level: level > at.z)
        self.guarded(step - 3 - (top - at.z), sink, lambda level: level < at.z)
        self.guarded(step - self.last, arrive, lambda level: level == at.z)

    def step(self, number):
        self.begin(number)
        self.first(number - 1)
        self.second(number - 2)
        self.along(number)

    def finish(self):
        at = self.at

        def loop(item, carry):
            def body(item, views, index, rows):
                for kind in range(5):
                    self.copy(views, kind, item).wait_send()

            self.guarded(item, body)
            self.guarded(
                item,
                lambda item, views, index, rows: self.copy(views, 5, item).wait_send(),
                lambda level: level > at.z,
            )
            self.guarded(
                item,
                lambda item, views, index, rows: self.copy(views, 6, item).wait_send(),
                lambda level: level < at.z,
            )
            return carry

        lax.fori_loop(0, self.count, loop, 0)


class Total:
    def __init__(self, at, sums, came, send, recv):
        self.at, self.sums, self.came, self.send, self.recv = at, sums, came, send, recv
        self.steps = 4 + at.levels

    def copy(self, kind, slot, device):
        return remote(
            self.sums.at[slot], self.came.at[kind], self.send.at[kind], self.recv.at[kind], device
        )

    def near(self, kind):
        at = self.at
        return self.copy(kind, kind, (at.pair, at.near_x, at.near_y)[kind])

    def sink(self):
        return self.copy(3, 4, self.at.down)

    def rise(self):
        return self.copy(4, 5, self.at.up)

    def step(self, number):
        at = self.at
        top = at.levels - 1
        for kind in range(3):

            @pl.when(number == kind)
            def _(kind=kind):
                if kind:
                    self.near(kind - 1).wait_recv()
                    self.sums[kind] = self.sums[kind - 1] + self.came[kind - 1]
                self.near(kind).start()

        @pl.when(number == 3)
        def _():
            self.near(2).wait_recv()
            total = self.sums[2] + self.came[2]
            self.sums[3] = total
            self.sums[4] = total
            self.sums[5] = total

        @pl.when((number == 4 + top - at.z) & at.has_down)
        def _():
            @pl.when(at.has_up)
            def _():
                self.sink().wait_recv()
                self.sums[4] = self.sums[3] + self.came[3]

            self.sink().start()

        @pl.when((number == 4 + at.z) & at.has_up)
        def _():
            @pl.when(at.has_down)
            def _():
                self.rise().wait_recv()
                self.sums[5] = self.sums[3] + self.came[4]

            self.rise().start()

    def finish(self, out_ref):
        at = self.at

        @pl.when(jnp.logical_not(at.has_down))
        def _():
            self.sink().wait_recv()

        @pl.when(jnp.logical_not(at.has_up))
        def _():
            self.rise().wait_recv()

        out_ref[...] = self.sums[3]

        @pl.when(at.has_up)
        def _():
            out_ref[...] = out_ref[...] + self.came[3]
            self.rise().wait_send()

        @pl.when(at.has_down)
        def _():
            out_ref[...] = out_ref[...] + self.came[4]
            self.sink().wait_send()

        for kind in range(3):
            self.near(kind).wait_send()


def total_scratch(rows):
    return [
        pltpu.VMEM((6, rows, 128), F32),
        pltpu.VMEM((5, rows, 128), F32),
        pltpu.SemaphoreType.DMA((5,)),
        pltpu.SemaphoreType.DMA((5,)),
    ]


def scatter_scratch(levels):
    items = levels * CHUNKS
    h = CHUNK // 2
    return [
        pltpu.VMEM((levels, 2, 2, SHARD, D), BF16),
        pltpu.VMEM((levels, 2, 2, SHARD, D), BF16),
        pltpu.VMEM((items, 2, h, D), BF16),
        pltpu.VMEM((items, 2, CHUNK - h, D), BF16),
        pltpu.VMEM((items, CHUNK - h, D), BF16),
        pltpu.VMEM((items, h, D), BF16),
        pltpu.VMEM((items, CHUNK, D), BF16),
        pltpu.VMEM((items, CHUNK, D), BF16),
        pltpu.SemaphoreType.DMA((7, items)),
        pltpu.SemaphoreType.DMA((7, items)),
        pltpu.SemaphoreType.DMA((items,)),
    ]


def vector_row(vec_ref, first, count=D):
    low = first // 128
    return jnp.concatenate([vec_ref[low + i : low + i + 1, :] for i in range(count // 128)], axis=1)


def rows_of(ref, first, count):
    return ref[...].reshape(-1, D)[first : first + count]


ROW_CHUNK = 256


def forward_call_kernel(
    own_ref,
    vec_ref,
    in_ref,
    bias_ref,
    x_ref,
    n_ref,
    q_ref,
    k_ref,
    v_ref,
    o_ref,
    lt_ref,
    w0_ref,
    w1_ref,
    vecs_ref,
    l_ref,
    send0,
    recv0,
    send1,
    recv1,
    misc_send,
    misc_recv,
    local_sem,
    *vec_scratch,
):
    at = Place()
    rows = x_ref.shape[0]
    slots = rows // 2
    kept = pltpu.make_async_copy(in_ref.at[at.y], x_ref.at[pl.ds(0, slots)], local_sem.at[0])
    kept.start()

    def own_copy():
        first = pltpu.make_async_copy(own_ref, w0_ref.at[0, at.x, at.y, at.c], local_sem.at[1])
        later = pltpu.make_async_copy(
            own_ref, w1_ref.at[jnp.maximum(at.z - 1, 0), at.x, at.y, at.c], local_sem.at[1]
        )
        return first, later

    first_own, later_own = own_copy()

    @pl.when(at.z == 0)
    def _():
        first_own.start()

    @pl.when(at.z > 0)
    def _():
        later_own.start()

    sums, came, vec_send, vec_recv = vec_scratch
    sums[0] = vec_ref[...]
    total = Total(at, sums, came, vec_send, vec_recv)
    first_own.wait()
    at.barrier()

    swap = remote(
        in_ref.at[1 - at.y],
        x_ref.at[pl.ds(slots, slots)],
        misc_send.at[0],
        misc_recv.at[0],
        at.near_y,
    )
    base = Gather(at, w0_ref, send0, recv0, 0, 0, 0)
    rest = Gather(at, w1_ref, send1, recv1, 1, at.levels - 1, 48)

    total.step(0)
    swap.start()
    for number in range(3):
        base.step(number)
    kept.wait()

    def early(number, carry):
        base.step(number)
        total.step(number - 2)
        return carry

    lax.fori_loop(3, 10, early, 0)
    total.step(8)
    total.finish(vecs_ref)
    for number in range(3):
        rest.column(number)
    swap.wait_recv()
    gain = vector_row(vecs_ref, 0)
    shift = vector_row(vecs_ref, D)
    for chunk in range(rows // ROW_CHUNK):
        part = pl.ds(chunk * ROW_CHUNK, ROW_CHUNK)
        n_ref[part, :] = layer_norm(x_ref[part, :].astype(F32), gain, shift).astype(BF16)

    def late(number, carry):
        base.step(number)
        return carry

    lax.fori_loop(10, base.steps, late, 0)
    base.finish()

    bias_query = vector_row(vecs_ref, 2 * D)
    bias_value = vector_row(vecs_ref, 3 * D)
    w_key = rows_of(w0_ref, D, D)
    for chunk in range(rows // ROW_CHUNK):
        part = pl.ds(chunk * ROW_CHUNK, ROW_CHUNK)
        k_ref[part, :] = matmul(n_ref[part, :], w_key).astype(BF16)
    mine, other = pl.ds(0, rows), pl.ds(rows, rows)
    key_copy = remote(k_ref.at[mine], k_ref.at[other], misc_send.at[1], misc_recv.at[1], at.pair)
    value_copy = remote(v_ref.at[mine], v_ref.at[other], misc_send.at[2], misc_recv.at[2], at.pair)
    key_copy.start()
    w_value = rows_of(w0_ref, 2 * D, D)
    for chunk in range(rows // ROW_CHUNK):
        part = pl.ds(chunk * ROW_CHUNK, ROW_CHUNK)
        v_ref[part, :] = (matmul(n_ref[part, :], w_value) + bias_value).astype(BF16)
    value_copy.start()
    w_query = rows_of(w0_ref, 0, D)
    for chunk in range(rows // ROW_CHUNK):
        part = pl.ds(chunk * ROW_CHUNK, ROW_CHUNK)
        query = (matmul(n_ref[part, :], w_query) + bias_query).astype(BF16)
        q_ref[part, :] = query * jnp.asarray(HEAD ** (-0.5), BF16)
    rest.plane(0)
    l_ref[...] = jnp.zeros_like(l_ref)
    key_copy.wait_recv()
    value_copy.wait_recv()

    def pair_step(pair, carry):
        forward_pair(pair, q_ref, k_ref, v_ref, bias_ref, o_ref, l_ref, ROW_CHUNK)
        for extra in range(2):
            number = 2 * pair + extra + 1

            @pl.when(number > 2)
            def _(number=number):
                rest.column(number)

            rest.plane(number - 0)
            rest.diagonal(number - 1)
        return carry

    def rest_step(number, carry):
        rest.column(number)
        rest.plane(number)
        rest.diagonal(number - 1)
        return carry

    lax.fori_loop(0, PAIRS, pair_step, 0)
    lt_ref[...] = l_ref[...].T[: lt_ref.shape[0]]
    lax.fori_loop(2 * PAIRS + 1, rest.steps, rest_step, 0)
    rest.finish()
    swap.wait_send()
    key_copy.wait_send()
    value_copy.wait_send()


def forward_call(own, vec_part, inputs, bias, levels):
    rows = inputs.shape[0] * inputs.shape[1]
    vmem = pl.BlockSpec(memory_space=pltpu.VMEM)
    anywhere = pl.BlockSpec(memory_space=pl.ANY)
    slots = levels * CHUNKS
    low = lambda *shape: jax.ShapeDtypeStruct(shape, BF16)
    return pl.pallas_call(
        forward_call_kernel,
        out_shape=(
            low(rows, D),
            low(rows, D),
            low(rows, D),
            low(2 * rows, D),
            low(2 * rows, D),
            low(rows, D),
            jax.ShapeDtypeStruct((16, rows), F32),
            low(1, 2, 2, 2, SHARD, D),
            low(levels - 1, 2, 2, 2, SHARD, D),
            jax.ShapeDtypeStruct(vec_part.shape, F32),
        ),
        in_specs=[anywhere, vmem, anywhere, vmem],
        out_specs=(vmem,) * 8 + (anywhere, vmem),
        scratch_shapes=[
            pltpu.VMEM((rows, LANES), F32),
            pltpu.SemaphoreType.DMA((11, slots)),
            pltpu.SemaphoreType.DMA((11, slots)),
            pltpu.SemaphoreType.DMA((11, slots)),
            pltpu.SemaphoreType.DMA((11, slots)),
            pltpu.SemaphoreType.DMA((3,)),
            pltpu.SemaphoreType.DMA((3,)),
            pltpu.SemaphoreType.DMA((2,)),
        ]
        + total_scratch(vec_part.shape[0]),
        compiler_params=pltpu.CompilerParams(
            collective_id=0, has_side_effects=True, vmem_limit_bytes=VMEM_LIMIT
        ),
        name="gather_attend",
    )(own, vec_part, inputs, bias)


def scatter_call_kernel(g_ref, vec_ref, out_ref, vecs_ref, *scratch):
    at = Place()
    sums, came, vec_send, vec_recv = scratch[11:]
    sums[0] = vec_ref[...]
    at.barrier()
    total = Total(at, sums, came, vec_send, vec_recv)
    scatter = Scatter(
        at, g_ref, out_ref, scratch[:8], scratch[8], scratch[9], scratch[10], 0, at.levels - 1
    )

    def step(number, carry):
        scatter.step(number)
        total.step(number)
        return carry

    lax.fori_loop(0, scatter.steps, step, 0)
    total.finish(vecs_ref)
    scatter.finish()


def scatter_call(grads, vec_part, levels):
    vmem = pl.BlockSpec(memory_space=pltpu.VMEM)
    anywhere = pl.BlockSpec(memory_space=pl.ANY)
    return pl.pallas_call(
        scatter_call_kernel,
        out_shape=(
            jax.ShapeDtypeStruct((SHARD, D), F32),
            jax.ShapeDtypeStruct(vec_part.shape, F32),
        ),
        in_specs=[anywhere, vmem],
        out_specs=(vmem, vmem),
        scratch_shapes=scatter_scratch(levels) + total_scratch(vec_part.shape[0]),
        compiler_params=pltpu.CompilerParams(
            collective_id=1, has_side_effects=True, vmem_limit_bytes=VMEM_LIMIT
        ),
        name="scatter_sum",
    )(grads, vec_part)


def plain_local(inputs, lengths, matrices, vectors, cotangent):
    seq_count, local_slots, width = inputs.shape
    tok_size = lax.axis_size("tok")
    tok = lax.axis_index("tok")
    half = tok // 2
    devices = tok_size * lax.axis_size("seq")
    rows = seq_count * local_slots
    across = [(i, (i + 2) % 4) for i in range(4)]
    partner = [(i, i + 1 - 2 * (i % 2)) for i in range(4)]

    def pick(array, index):
        return lax.dynamic_index_in_dim(array, index, 0, keepdims=False)

    def to_sequence(array):
        other = lax.ppermute(pick(array, 1 - half), "tok", across)
        return jnp.concatenate([pick(array, half), other], axis=0)

    def from_sequence(array):
        other = lax.ppermute(array[local_slots:], "tok", across)
        kept = array[:local_slots]
        return jnp.where(half == 0, jnp.stack([kept, other]), jnp.stack([other, kept]))

    shard_rows = matrices.shape[0] // width
    low_rows = matrices.reshape(shard_rows, width).astype(BF16)
    gathered = lax.all_gather(low_rows, ("seq", "tok"), axis=0, tiled=True)
    w_query, w_key, w_value, w_out, w_up, w_down = split_matrices(gathered)
    vec_count = vectors.shape[0]
    vec_rows = 8
    vec_pad = vec_rows * 128 - vec_count
    vec_low = jnp.pad(vectors, (0, vec_pad)).astype(BF16).reshape(vec_rows, 128)
    vecs = lax.all_gather(vec_low, ("seq", "tok"), axis=0, tiled=True)
    vecs = vecs.reshape(devices, vec_rows * 128)[:, :vec_count].reshape(-1)
    (
        gain_one,
        first_norm_shift,
        bias_query,
        bias_value,
        bias_out,
        gain_two,
        shift_two,
        bias_up,
        bias_down,
    ) = split_vectors(vecs.astype(F32))

    token_rows = to_sequence(inputs).astype(F32)
    grad_out = to_sequence(cotangent)
    length = pick(lengths, half)
    slot = jnp.arange(local_slots, dtype=jnp.int32)
    places = jnp.concatenate([block * local_slots + slot for block in (tok, tok ^ 2, tok ^ 1, tok ^ 3)])
    bias = jnp.where(places < length, 0.0, -1e30).astype(BF16)[:, None]
    bias = jnp.broadcast_to(bias, (bias.shape[0], LANES))

    normed = layer_norm(token_rows, gain_one, first_norm_shift).astype(BF16)
    query = (matmul(normed, w_query) + bias_query).astype(BF16)
    scaled = query * jnp.asarray(HEAD ** (-0.5), BF16)
    keys_here = matmul(normed, w_key).astype(BF16)
    values_here = (matmul(normed, w_value) + bias_value).astype(BF16)
    keys = jnp.concatenate([keys_here, lax.ppermute(keys_here, "tok", partner)], axis=0)
    values = jnp.concatenate([values_here, lax.ppermute(values_here, "tok", partner)], axis=0)
    attended, lt = attend(scaled, keys, values, bias)
    middle = token_rows + (matmul(attended, w_out) + bias_out)
    normed_two = layer_norm(middle, gain_two, shift_two).astype(BF16)
    hidden = matmul(normed_two, w_up) + bias_up
    active = jax.nn.gelu(hidden, approximate=False).astype(BF16)
    result = middle + (matmul(active, w_down) + bias_down)
    outputs = from_sequence(result.astype(BF16))

    grad_out_wide = grad_out.astype(F32)
    d_down = outer_sum(active, grad_out)
    down_bias_gradient = column_sum(grad_out)
    grad_active = back_product(grad_out, w_down)
    gelu_value, gelu_pull = jax.vjp(partial(jax.nn.gelu, approximate=False), hidden)
    grad_hidden = gelu_pull(grad_active)[0].astype(BF16)
    d_up = outer_sum(normed_two, grad_hidden)
    d_bias_up = column_sum(grad_hidden)
    grad_normed_two = back_product(grad_hidden, w_up)
    norm_value, norm_pull = jax.vjp(layer_norm, middle, gain_two, shift_two)
    grad_mid_norm, d_gain_two, d_shift_two = norm_pull(grad_normed_two)
    grad_middle = grad_out_wide + grad_mid_norm
    grad_branch = grad_middle.astype(BF16)
    d_out = outer_sum(attended, grad_branch)
    d_bias_out = column_sum(grad_branch)
    grad_attended = back_product(grad_branch, w_out).astype(BF16)
    inner = (grad_attended.astype(F32) * attended.astype(F32)).reshape(rows, HEADS, HEAD).sum(-1)
    inner = jnp.pad(inner.T, ((0, 16 - HEADS), (0, 0)))
    grad_query, grad_keys, grad_values = attend_back(
        scaled, keys, values, bias, grad_attended, lt, inner
    )

    def pair_sum(array):
        other = lax.ppermute(array[rows:], "tok", partner)
        return (array[:rows].astype(F32) + other.astype(F32)).astype(BF16)

    grad_key = pair_sum(grad_keys)
    grad_value = pair_sum(grad_values)
    d_query = outer_sum(normed, grad_query)
    d_key = outer_sum(normed, grad_key)
    d_value = outer_sum(normed, grad_value)
    d_bias_query = column_sum(grad_query)
    d_bias_value = column_sum(grad_value)
    grad_normed = (
        back_product(grad_query, w_query)
        + back_product(grad_key, w_key)
        + back_product(grad_value, w_value)
    )
    first_value, leading_pullback = jax.vjp(layer_norm, token_rows, gain_one, first_norm_shift)
    grad_rows_norm, d_gain_one, d_shift_one = leading_pullback(grad_normed)
    grad_inputs = from_sequence((grad_middle + grad_rows_norm).astype(BF16))
    matrix_rows = jnp.concatenate(
        [
            piece.astype(BF16).reshape(-1, width)
            for piece in (d_query, d_key, d_value, d_out, d_up, d_down)
        ]
    )
    flat_vector_grads = jnp.concatenate(
        [
            d_gain_one,
            d_shift_one,
            d_bias_query,
            d_bias_value,
            d_bias_out,
            d_gain_two,
            d_shift_two,
            d_bias_up,
            down_bias_gradient,
        ]
    )
    vector_rows = jnp.pad(flat_vector_grads.reshape(devices, vec_count), ((0, 0), (0, vec_pad)))
    grad_rows = lax.psum_scatter(
        matrix_rows, ("seq", "tok"), scatter_dimension=0, tiled=True
    )
    grad_vec_rows = lax.psum_scatter(
        vector_rows.reshape(devices * vec_rows, 128), ("seq", "tok"), scatter_dimension=0, tiled=True
    )
    grad_matrices = grad_rows.astype(F32).reshape(-1)
    grad_vectors = grad_vec_rows.reshape(-1)[:vec_count]
    return (outputs, grad_inputs, grad_matrices, grad_vectors)


def fast_local(inputs, lengths, matrices, vectors, cotangent):
    seq_count, local_slots, width = inputs.shape
    tok = lax.axis_index("tok")
    half = tok // 2
    place = lax.axis_index("seq") * lax.axis_size("tok") + tok
    levels = lax.axis_size("seq") // 2
    devices = lax.axis_size("seq") * lax.axis_size("tok")
    rows = seq_count * local_slots
    across = [(i, (i + 2) % 4) for i in range(4)]
    partner = [(i, i + 1 - 2 * (i % 2)) for i in range(4)]

    def pick(array, index):
        return lax.dynamic_index_in_dim(array, index, 0, keepdims=False)

    def to_sequence(array):
        other = lax.ppermute(pick(array, 1 - half), "tok", across)
        return jnp.concatenate([pick(array, half), other], axis=0)

    def from_sequence(array):
        other = lax.ppermute(array[local_slots:], "tok", across)
        kept = array[:local_slots]
        return jnp.where(half == 0, jnp.stack([kept, other]), jnp.stack([other, kept]))

    own = matrices.reshape(SHARD, width).astype(BF16)
    vec_count = vectors.shape[0]
    vec_total = vec_count * devices
    vec_part = lax.dynamic_update_slice(
        jnp.zeros((vec_total,), F32), vectors.astype(BF16).astype(F32), (place * vec_count,)
    ).reshape(vec_total // 128, 128)
    length = pick(lengths, half)
    slot = jnp.arange(local_slots, dtype=jnp.int32)
    places = jnp.concatenate(
        [block * local_slots + slot for block in (tok, tok ^ 2, tok ^ 1, tok ^ 3)]
    )
    bias = jnp.where(places < length, 0.0, -1e30).astype(BF16)[:, None]
    bias = jnp.broadcast_to(bias, (bias.shape[0], LANES))
    frames, normed, scaled, keys, values, attended, lt, w_first, w_rest, vecs = forward_call(
        own, vec_part, inputs, bias, levels
    )
    grad_out = to_sequence(cotangent)
    (
        gain_one,
        first_norm_shift,
        bias_query,
        bias_value,
        bias_out,
        gain_two,
        shift_two,
        bias_up,
        bias_down,
    ) = split_vectors(vecs.reshape(-1))
    first_rows = w_first.reshape(-1, width)
    w_query, w_key, w_value = (first_rows[i * D : (i + 1) * D] for i in range(3))
    rest_rows = w_rest.reshape(-1, width)
    w_out = rest_rows[:D]
    w_up = rest_rows[D : D + FF].reshape(D, FF)
    w_down = rest_rows[D + FF : D + 2 * FF]
    token_rows = frames.astype(F32)
    middle = token_rows + (matmul(attended, w_out) + bias_out)
    normed_two = layer_norm(middle, gain_two, shift_two).astype(BF16)
    hidden = matmul(normed_two, w_up) + bias_up
    active = jax.nn.gelu(hidden, approximate=False).astype(BF16)
    result = middle + (matmul(active, w_down) + bias_down)
    outputs = from_sequence(result.astype(BF16))

    grad_out_wide = grad_out.astype(F32)
    d_down = outer_sum(active, grad_out)
    down_bias_gradient = column_sum(grad_out)
    grad_active = back_product(grad_out, w_down)
    gelu_value, gelu_pull = jax.vjp(partial(jax.nn.gelu, approximate=False), hidden)
    grad_hidden = gelu_pull(grad_active)[0].astype(BF16)
    d_up = outer_sum(normed_two, grad_hidden)
    d_bias_up = column_sum(grad_hidden)
    grad_normed_two = back_product(grad_hidden, w_up)
    norm_value, norm_pull = jax.vjp(layer_norm, middle, gain_two, shift_two)
    grad_mid_norm, d_gain_two, d_shift_two = norm_pull(grad_normed_two)
    grad_middle = grad_out_wide + grad_mid_norm
    grad_branch = grad_middle.astype(BF16)
    d_out = outer_sum(attended, grad_branch)
    d_bias_out = column_sum(grad_branch)
    grad_attended = back_product(grad_branch, w_out).astype(BF16)
    inner = (grad_attended.astype(F32) * attended.astype(F32)).reshape(rows, HEADS, HEAD).sum(-1)
    inner = jnp.pad(inner.T, ((0, 16 - HEADS), (0, 0)))
    grad_query, grad_keys, grad_values = attend_back(
        scaled, keys, values, bias, grad_attended, lt, inner
    )

    def pair_sum(array):
        other = lax.ppermute(array[rows:], "tok", partner)
        return (array[:rows].astype(F32) + other.astype(F32)).astype(BF16)

    grad_key = pair_sum(grad_keys)
    grad_value = pair_sum(grad_values)
    d_query = outer_sum(normed, grad_query)
    d_key = outer_sum(normed, grad_key)
    d_value = outer_sum(normed, grad_value)
    d_bias_query = column_sum(grad_query)
    d_bias_value = column_sum(grad_value)
    grad_normed = (
        back_product(grad_query, w_query)
        + back_product(grad_key, w_key)
        + back_product(grad_value, w_value)
    )
    first_value, leading_pullback = jax.vjp(layer_norm, token_rows, gain_one, first_norm_shift)
    grad_rows_norm, d_gain_one, d_shift_one = leading_pullback(grad_normed)
    grad_inputs = from_sequence((grad_middle + grad_rows_norm).astype(BF16))
    matrix_rows = jnp.concatenate(
        [
            piece.astype(BF16).reshape(-1, width)
            for piece in (d_query, d_key, d_value, d_out, d_up, d_down)
        ]
    )
    flat_vector_grads = jnp.concatenate(
        [
            d_gain_one,
            d_shift_one,
            d_bias_query,
            d_bias_value,
            d_bias_out,
            d_gain_two,
            d_shift_two,
            d_bias_up,
            down_bias_gradient,
        ]
    )
    grad_rows, grad_vecs = scatter_call(
        matrix_rows.reshape(levels, 2, 2, 2, SHARD, width),
        flat_vector_grads.reshape(vec_part.shape),
        levels,
    )
    grad_matrices = grad_rows.reshape(-1)
    grad_vectors = lax.dynamic_slice(grad_vecs.reshape(-1), (place * vec_count,), (vec_count,))
    return (outputs, grad_inputs, grad_matrices, grad_vectors)


def solution(mesh):
    seq_size, tok_size = mesh.shape["seq"], mesh.shape["tok"]
    in_specs = (
        P("seq", "tok", None),
        P("seq"),
        P(("seq", "tok")),
        P(("seq", "tok")),
        P("seq", "tok", None),
    )
    out_specs = (P("seq", "tok", None), P("seq", "tok", None), P(("seq", "tok")), P(("seq", "tok")))
    whole_rows = (4 * D + 2 * FF) == seq_size * tok_size * SHARD
    body = fast_local if whole_rows and tok_size == 4 else plain_local
    return jax.shard_map(body, mesh=mesh, in_specs=in_specs, out_specs=out_specs, check_vma=False)
```

```python
from functools import partial

import jax
import jax.numpy as jnp
from jax import lax
from jax.experimental import pallas as pl
from jax.experimental.pallas import tpu as pltpu
from jax.sharding import PartitionSpec as P

D = 768
HEADS = 12
HEAD = 64
FF = 3072
PAIRS = HEADS // 2
LANES = 2 * HEAD
F32 = jnp.float32
BF16 = jnp.bfloat16
VMEM_LIMIT = 56 * 1024 * 1024


def layer_norm(token_rows, norm_gain, norm_shift):
    center = jnp.mean(token_rows, axis=-1, keepdims=True)
    centered = token_rows - center
    spread = jnp.mean(centered * centered, axis=-1, keepdims=True)
    return centered * lax.rsqrt(spread + 1e-05) * norm_gain + norm_shift


def matmul(left_operand, right_operand):
    return jnp.dot(left_operand, right_operand, preferred_element_type=F32)


def outer_sum(left_operand, right_operand):
    return lax.dot_general(
        left_operand, right_operand, (((0,), (0,)), ((), ())), preferred_element_type=F32
    )


def back_product(gradient, weight):
    return lax.dot_general(
        gradient, weight, (((1,), (1,)), ((), ())), preferred_element_type=F32
    )


def column_sum(gradient):
    return jnp.sum(gradient.astype(F32), axis=0)


def pair_columns(pair):
    return pl.ds(pl.multiple_of(pair * LANES, LANES), LANES)


def forward_pair(pair, q_ref, k_ref, v_ref, bias_ref, o_ref, l_ref, row_chunk):
    rows = q_ref.shape[0]
    keys = k_ref.shape[0]
    cols = pair_columns(pair)
    lane_k = lax.broadcasted_iota(jnp.int32, (keys, LANES), 1)
    lane_q = lax.broadcasted_iota(jnp.int32, (row_chunk, LANES), 1)
    lane_l = lax.broadcasted_iota(jnp.int32, (row_chunk, LANES), 1)
    key_pair = k_ref[:, cols]
    value_pair = v_ref[:, cols]
    bias = bias_ref[...]
    head_keys = []
    for half in range(2):
        own = lane_k // HEAD == half
        spare = lane_k == (1 - half) * HEAD
        head_keys.append(jnp.where(own, key_pair, jnp.where(spare, bias, jnp.zeros_like(bias))))
    for chunk in range(rows // row_chunk):
        part = pl.ds(chunk * row_chunk, row_chunk)
        query_pair = q_ref[part, cols]
        one = jnp.ones_like(query_pair)
        results = []
        masses = l_ref[part, :]
        for half in range(2):
            own_q = lane_q // HEAD == half
            query = jnp.where(own_q, query_pair, one)
            scores = lax.dot_general(
                query, head_keys[half], (((1,), (1,)), ((), ())), preferred_element_type=F32
            )
            peak = jnp.max(scores, axis=-1, keepdims=True)
            raised = jnp.exp(scores - peak)
            mass = jnp.sum(raised, axis=-1, keepdims=True)
            soft = (raised * (1.0 / mass)).astype(BF16)
            results.append(matmul(soft, value_pair))
            masses = jnp.where(lane_l == 2 * pair + half, peak + jnp.log(mass), masses)
        l_ref[part, :] = masses
        o_ref[part, cols] = jnp.where(lane_q // HEAD == 0, results[0], results[1]).astype(BF16)


def forward_kernel(row_chunk, q_ref, k_ref, v_ref, bias_ref, o_ref, lt_ref, l_ref):
    l_ref[...] = jnp.zeros_like(l_ref)

    def step(pair, carry):
        forward_pair(pair, q_ref, k_ref, v_ref, bias_ref, o_ref, l_ref, row_chunk)
        return carry

    lax.fori_loop(0, PAIRS, step, 0)
    lt_ref[...] = l_ref[...].T[: lt_ref.shape[0]]


def attend(query, keys, values, bias):
    rows = query.shape[0]
    vmem = pl.BlockSpec(memory_space=pltpu.VMEM)
    return pl.pallas_call(
        partial(forward_kernel, 256),
        out_shape=(
            jax.ShapeDtypeStruct((rows, D), BF16),
            jax.ShapeDtypeStruct((16, rows), F32),
        ),
        in_specs=[vmem] * 4,
        out_specs=(vmem, vmem),
        scratch_shapes=[pltpu.VMEM((rows, LANES), F32)],
        compiler_params=pltpu.CompilerParams(vmem_limit_bytes=VMEM_LIMIT),
        name="attend",
    )(query, keys, values, bias)


def backward_pair(
    pair, q_ref, k_ref, v_ref, bias_ref, g_ref, lt_ref, dt_ref, dq_ref, dk_ref, dv_ref, key_chunk
):
    rows = q_ref.shape[0]
    keys = k_ref.shape[0]
    cols = pair_columns(pair)
    lane_k = lax.broadcasted_iota(jnp.int32, (key_chunk, LANES), 1)
    lane_q = lax.broadcasted_iota(jnp.int32, (rows, LANES), 1)
    query_pair = q_ref[:, cols]
    grad_pair = g_ref[:, cols]
    one = jnp.ones_like(query_pair)
    query_heads = [jnp.where(lane_q // HEAD == half, query_pair, one) for half in range(2)]
    zero = jnp.zeros((key_chunk, LANES), BF16)
    grad_query = [jnp.zeros((rows, LANES), F32) for _ in range(2)]
    for chunk in range(keys // key_chunk):
        part = pl.ds(chunk * key_chunk, key_chunk)
        key_pair = k_ref[part, cols]
        value_pair = v_ref[part, cols]
        bias = bias_ref[part, :]
        grad_key = []
        grad_value = []
        for half in range(2):
            own = lane_k // HEAD == half
            spare = lane_k == (1 - half) * HEAD
            head_key = jnp.where(own, key_pair, jnp.where(spare, bias, jnp.zeros_like(bias)))
            head_value = jnp.where(own, value_pair, zero)
            scores = back_product(head_key, query_heads[half])
            mass = lt_ref[pl.ds(2 * pair + half, 1), :]
            inner = dt_ref[pl.ds(2 * pair + half, 1), :]
            soft = jnp.exp(scores - mass)
            grad_soft = back_product(head_value, grad_pair)
            grad_scores = (soft * (grad_soft - inner)).astype(BF16)
            grad_value.append(matmul(soft.astype(BF16), grad_pair))
            grad_key.append(matmul(grad_scores, query_pair))
            grad_query[half] = grad_query[half] + outer_sum(grad_scores, key_pair)
        first = lane_k // HEAD == 0
        dk_ref[part, cols] = jnp.where(first, grad_key[0], grad_key[1]).astype(BF16)
        dv_ref[part, cols] = jnp.where(first, grad_value[0], grad_value[1]).astype(BF16)
    merged = jnp.where(lane_q // HEAD == 0, grad_query[0], grad_query[1])
    dq_ref[:, cols] = (merged * HEAD ** (-0.5)).astype(BF16)


def backward_kernel(key_chunk, *refs):
    def step(pair, carry):
        backward_pair(pair, *refs, key_chunk)
        return carry

    lax.fori_loop(0, PAIRS, step, 0)


def attend_back(query, keys, values, bias, grad, lt, dt):
    vmem = pl.BlockSpec(memory_space=pltpu.VMEM)
    return pl.pallas_call(
        partial(backward_kernel, 256),
        out_shape=(
            jax.ShapeDtypeStruct(query.shape, BF16),
            jax.ShapeDtypeStruct(keys.shape, BF16),
            jax.ShapeDtypeStruct(keys.shape, BF16),
        ),
        in_specs=[vmem] * 7,
        out_specs=(vmem,) * 3,
        compiler_params=pltpu.CompilerParams(vmem_limit_bytes=VMEM_LIMIT),
        name="attend_back",
    )(query, keys, values, bias, grad, lt, dt)


def split_matrices(rows):
    w_up = rows[4 * D : 4 * D + FF].reshape(D, FF)
    w_down = rows[4 * D + FF : 4 * D + 2 * FF]
    return (rows[:D], rows[D : 2 * D], rows[2 * D : 3 * D], rows[3 * D : 4 * D], w_up, w_down)


def split_vectors(flattened):
    pieces = []
    for number in range(7):
        pieces.append(flattened[number * D : (number + 1) * D])
    pieces.append(flattened[7 * D : 7 * D + FF])
    pieces.append(flattened[7 * D + FF : 8 * D + FF])
    return tuple(pieces)


SHARD = 288
CHUNKS = 3
CHUNK = SHARD // CHUNKS
MESH = pl.DeviceIdType.MESH
UP, DOWN, NEAR_X, NEAR_Y, DIAG_A, DIAG_B, PAIR_C, PAIR_X, PAIR_Y, PAIR_A, PAIR_B = range(11)


class Place:
    def __init__(self):
        self.seq = lax.axis_index("seq")
        self.tok = lax.axis_index("tok")
        self.z = self.seq // 2
        self.x = self.seq % 2
        self.y = self.tok // 2
        self.c = self.tok % 2
        self.levels = lax.axis_size("seq") // 2
        self.up = (self.seq + 2, self.tok)
        self.down = (self.seq - 2, self.tok)
        self.near_x = (self.seq + 1 - 2 * self.x, self.tok)
        self.near_y = (self.seq, self.tok + 2 - 4 * self.y)
        self.pair = (self.seq, self.tok + 1 - 2 * self.c)
        self.has_up = self.z < self.levels - 1
        self.has_down = self.z > 0

    def barrier(self):
        sem = pltpu.get_barrier_semaphore()
        for device in (self.near_x, self.near_y, self.pair):
            pl.semaphore_signal(sem, inc=1, device_id=device, device_id_type=MESH)

        @pl.when(self.has_up)
        def _():
            pl.semaphore_signal(sem, inc=1, device_id=self.up, device_id_type=MESH)

        @pl.when(self.has_down)
        def _():
            pl.semaphore_signal(sem, inc=1, device_id=self.down, device_id_type=MESH)

        count = 3 + self.has_up.astype(jnp.int32) + self.has_down.astype(jnp.int32)
        pl.semaphore_wait(sem, count)


def remote(source, target, send, recv, device):
    return pltpu.make_async_remote_copy(
        src_ref=source,
        dst_ref=target,
        send_sem=send,
        recv_sem=recv,
        device_id=device,
        device_id_type=MESH,
    )


class Gather:
    def __init__(self, at, w_ref, send, recv, low, high, split):
        self.at, self.w, self.send, self.recv = at, w_ref, send, recv
        self.low, self.high, self.split = low, high, split
        self.steps = at.levels * CHUNKS + 2

    def piece(self, level, x, y, c, first, count):
        first = pl.multiple_of(first, 16)
        return self.w.at[level - self.low, x, y, c, pl.ds(first, count)]

    def copies(self, level, chunk):
        at, split = self.at, self.split
        x, y, c = at.x, at.y, at.c
        first = chunk * CHUNK

        def view(xs, ys, cs, low=0, count=CHUNK):
            return self.piece(level, xs, ys, cs, first + low, count)

        rest = CHUNK - split
        table = {
            UP: (view(x, y, c), view(x, y, c), at.up),
            DOWN: (view(x, y, c), view(x, y, c), at.down),
            NEAR_X: (view(x, y, c), view(1 - x, y, c), at.near_x),
            NEAR_Y: (view(x, y, c), view(x, 1 - y, c), at.near_y),
            PAIR_C: (view(x, y, c), view(x, y, 1 - c), at.pair),
            PAIR_X: (view(1 - x, y, c), view(1 - x, y, 1 - c), at.pair),
            PAIR_Y: (view(x, 1 - y, c), view(x, 1 - y, 1 - c), at.pair),
        }
        if split:
            table[DIAG_A] = (
                view(1 - x, y, c, 0, split),
                view(1 - x, 1 - y, c, 0, split),
                at.near_y,
            )
            table[PAIR_A] = (
                view(1 - x, 1 - y, c, 0, split),
                view(1 - x, 1 - y, 1 - c, 0, split),
                at.pair,
            )
        if rest:
            table[DIAG_B] = (
                view(x, 1 - y, c, split, rest),
                view(1 - x, 1 - y, c, split, rest),
                at.near_x,
            )
            table[PAIR_B] = (
                view(1 - x, 1 - y, c, split, rest),
                view(1 - x, 1 - y, 1 - c, split, rest),
                at.pair,
            )
        return table

    def start(self, table, kind, slot):
        sent, _, device = table[kind]
        remote(sent, sent, self.send.at[kind, slot], self.recv.at[kind, slot], device).start()

    def wait_recv(self, table, kind, slot):
        _, came, device = table[kind]
        remote(came, came, self.send.at[kind, slot], self.recv.at[kind, slot], device).wait_recv()

    def wait_send(self, table, kind, slot):
        sent, _, device = table[kind]
        remote(sent, sent, self.send.at[kind, slot], self.recv.at[kind, slot], device).wait_send()

    def items(self, index, body):
        at = self.at
        inside = (index >= 0) & (index < at.levels * CHUNKS)
        distance = jnp.where(inside, index // CHUNKS, 0)
        chunk = jnp.where(inside, index % CHUNKS, 0)
        for below in (True, False):
            level = at.z - distance if below else at.z + distance
            valid = inside & (level >= self.low) & (level <= self.high)
            if not below:
                valid = valid & (distance > 0)

            @pl.when(valid)
            def _(level=level, below=below):
                slot = level * CHUNKS + chunk
                body(slot, self.copies(level, chunk), distance == 0, below)

    def column(self, index):
        at = self.at

        def body(slot, table, own, below):
            @pl.when(jnp.logical_not(own))
            def _():
                self.wait_recv(table, UP if below else DOWN, slot)

            if below:

                @pl.when(at.has_up)
                def _():
                    self.start(table, UP, slot)

                @pl.when(own & at.has_down)
                def _():
                    self.start(table, DOWN, slot)

            else:

                @pl.when(at.has_down)
                def _():
                    self.start(table, DOWN, slot)

            for kind in (NEAR_Y, NEAR_X, PAIR_C):
                self.start(table, kind, slot)

        self.items(index, body)

    def plane(self, index):
        def body(slot, table, own, below):
            self.wait_recv(table, NEAR_Y, slot)
            for kind in (DIAG_B, PAIR_Y):
                if kind in table:
                    self.start(table, kind, slot)
            self.wait_recv(table, NEAR_X, slot)
            for kind in (DIAG_A, PAIR_X):
                if kind in table:
                    self.start(table, kind, slot)

        self.items(index, body)

    def diagonal(self, index):
        def body(slot, table, own, below):
            for kind, onward in ((DIAG_B, PAIR_B), (DIAG_A, PAIR_A)):
                if kind in table:
                    self.wait_recv(table, kind, slot)
                    self.start(table, onward, slot)

        self.items(index, body)

    def step(self, number):
        self.column(number)
        self.plane(number - 1)
        self.diagonal(number - 2)

    def finish(self):
        at = self.at

        def body(slot, table, own, below):
            for kind in (PAIR_C, PAIR_X, PAIR_Y, PAIR_A, PAIR_B):
                if kind in table:
                    self.wait_recv(table, kind, slot)
            if below:

                @pl.when(at.has_up)
                def _():
                    self.wait_send(table, UP, slot)

                @pl.when(own & at.has_down)
                def _():
                    self.wait_send(table, DOWN, slot)

            else:

                @pl.when(at.has_down)
                def _():
                    self.wait_send(table, DOWN, slot)

            for kind in table:
                if kind not in (UP, DOWN):
                    self.wait_send(table, kind, slot)

        def loop(index, carry):
            self.items(index, body)
            return carry

        lax.fori_loop(0, at.levels * CHUNKS, loop, 0)


class Scatter:
    def __init__(self, at, g_ref, out_ref, buffers, send, recv, local_sem, low, high):
        self.at, self.g, self.out, self.send, self.recv = at, g_ref, out_ref, send, recv
        self.acc, self.stage, self.x1, self.y1, self.x2, self.y2, self.za, self.zb = buffers
        self.local_sem, self.low, self.high = local_sem, low, high
        self.count = (high - low + 1) * CHUNKS
        self.last = at.levels + 2
        self.steps = self.count + self.last

    def half(self):
        return CHUNK // 2

    def views(self, item):
        at = self.at
        x, y, c = at.x, at.y, at.c
        index = item // CHUNKS
        first = pl.multiple_of((item % CHUNKS) * CHUNK, 16)
        h = self.half()
        rows = pl.ds(first, CHUNK)
        rows_a = pl.ds(first, h)
        rows_b = pl.ds(pl.multiple_of(first + h, 16), CHUNK - h)
        acc = self.acc
        mine = acc.at[index, x, y, rows]
        return {
            0: (self.g.at[index, :, :, 1 - c, rows], acc.at[index, :, :, rows], at.pair),
            1: (acc.at[index, 1 - x, :, rows_a], self.x1.at[item], at.near_x),
            2: (acc.at[index, :, 1 - y, rows_b], self.y1.at[item], at.near_y),
            3: (acc.at[index, x, 1 - y, rows_a], self.y2.at[item], at.near_y),
            4: (acc.at[index, 1 - x, y, rows_b], self.x2.at[item], at.near_x),
            5: (mine, self.zb.at[item], at.up),
            6: (mine, self.za.at[item], at.down),
        }, index, (rows, rows_a, rows_b)

    def copy(self, views, kind, item):
        source, target, device = views[kind]
        return remote(source, target, self.send.at[kind, item], self.recv.at[kind, item], device)

    def guarded(self, item, body, extra=None):
        valid = (item >= 0) & (item < self.count)
        item = jnp.where(valid, item, 0)
        level = self.low + item // CHUNKS
        if extra is not None:
            valid = valid & extra(level)

        @pl.when(valid)
        def _():
            views, index, rows = self.views(item)
            body(item, views, index, rows)

    def local(self, item, index, rows):
        return pltpu.make_async_copy(
            self.g.at[index, :, :, self.at.c, rows[0]],
            self.stage.at[item % 2],
            self.local_sem.at[item],
        )

    def begin(self, item):
        def body(item, views, index, rows):
            self.copy(views, 0, item).start()
            self.local(item, index, rows).start()

        self.guarded(item, body)

    @staticmethod
    def add(target, where, addend):
        target[where] = (target[where].astype(F32) + addend.astype(F32)).astype(BF16)

    def first(self, item):
        def body(item, views, index, rows):
            self.copy(views, 0, item).wait_recv()
            self.local(item, index, rows).wait()
            for xs in range(2):
                for ys in range(2):
                    where = (index, xs, ys, rows[0])
                    self.add(self.acc, where, self.stage[item % 2, xs, ys])
            self.copy(views, 1, item).start()
            self.copy(views, 2, item).start()

        self.guarded(item, body)

    def second(self, item):
        at = self.at

        def body(item, views, index, rows):
            self.copy(views, 1, item).wait_recv()
            for ys in range(2):
                self.add(self.acc, (index, at.x, ys, rows[1]), self.x1[item, ys])
            self.copy(views, 3, item).start()
            self.copy(views, 2, item).wait_recv()
            for xs in range(2):
                self.add(self.acc, (index, xs, at.y, rows[2]), self.y1[item, xs])
            self.copy(views, 4, item).start()

        self.guarded(item, body)

    def collect(self, item, views, index, rows):
        at = self.at
        self.copy(views, 3, item).wait_recv()
        self.copy(views, 4, item).wait_recv()
        self.add(self.acc, (index, at.x, at.y, rows[1]), self.y2[item])
        self.add(self.acc, (index, at.x, at.y, rows[2]), self.x2[item])

    def along(self, step):
        at = self.at

        def rise(item, views, index, rows):
            self.collect(item, views, index, rows)

            @pl.when(at.has_down)
            def _():
                self.copy(views, 5, item).wait_recv()
                self.add(self.acc, (index, at.x, at.y, rows[0]), self.zb[item])

            self.copy(views, 5, item).start()

        def sink(item, views, index, rows):
            self.collect(item, views, index, rows)

            @pl.when(at.has_up)
            def _():
                self.copy(views, 6, item).wait_recv()
                self.add(self.acc, (index, at.x, at.y, rows[0]), self.za[item])

            self.copy(views, 6, item).start()

        def arrive(item, views, index, rows):
            self.collect(item, views, index, rows)
            self.out[rows[0]] = self.acc[index, at.x, at.y, rows[0]].astype(F32)

            @pl.when(at.has_down)
            def _():
                self.copy(views, 5, item).wait_recv()
                self.out[rows[0]] = self.out[rows[0]] + self.zb[item].astype(F32)

            @pl.when(at.has_up)
            def _():
                self.copy(views, 6, item).wait_recv()
                self.out[rows[0]] = self.out[rows[0]] + self.za[item].astype(F32)

        top = at.levels - 1
        self.guarded(step - 3 - at.z, rise, lambda level: level > at.z)
        self.guarded(step - 3 - (top - at.z), sink, lambda level: level < at.z)
        self.guarded(step - self.last, arrive, lambda level: level == at.z)

    def step(self, number):
        self.begin(number)
        self.first(number - 1)
        self.second(number - 2)
        self.along(number)

    def finish(self):
        at = self.at

        def loop(item, carry):
            def body(item, views, index, rows):
                for kind in range(5):
                    self.copy(views, kind, item).wait_send()

            self.guarded(item, body)
            self.guarded(
                item,
                lambda item, views, index, rows: self.copy(views, 5, item).wait_send(),
                lambda level: level > at.z,
            )
            self.guarded(
                item,
                lambda item, views, index, rows: self.copy(views, 6, item).wait_send(),
                lambda level: level < at.z,
            )
            return carry

        lax.fori_loop(0, self.count, loop, 0)


class Total:
    def __init__(self, at, sums, came, send, recv):
        self.at, self.sums, self.came, self.send, self.recv = at, sums, came, send, recv
        self.steps = 4 + at.levels

    def copy(self, kind, slot, device):
        return remote(
            self.sums.at[slot], self.came.at[kind], self.send.at[kind], self.recv.at[kind], device
        )

    def near(self, kind):
        at = self.at
        return self.copy(kind, kind, (at.pair, at.near_x, at.near_y)[kind])

    def sink(self):
        return self.copy(3, 4, self.at.down)

    def rise(self):
        return self.copy(4, 5, self.at.up)

    def step(self, number):
        at = self.at
        top = at.levels - 1
        for kind in range(3):

            @pl.when(number == kind)
            def _(kind=kind):
                if kind:
                    self.near(kind - 1).wait_recv()
                    self.sums[kind] = self.sums[kind - 1] + self.came[kind - 1]
                self.near(kind).start()

        @pl.when(number == 3)
        def _():
            self.near(2).wait_recv()
            total = self.sums[2] + self.came[2]
            self.sums[3] = total
            self.sums[4] = total
            self.sums[5] = total

        @pl.when((number == 4 + top - at.z) & at.has_down)
        def _():
            @pl.when(at.has_up)
            def _():
                self.sink().wait_recv()
                self.sums[4] = self.sums[3] + self.came[3]

            self.sink().start()

        @pl.when((number == 4 + at.z) & at.has_up)
        def _():
            @pl.when(at.has_down)
            def _():
                self.rise().wait_recv()
                self.sums[5] = self.sums[3] + self.came[4]

            self.rise().start()

    def finish(self, out_ref):
        at = self.at

        @pl.when(jnp.logical_not(at.has_down))
        def _():
            self.sink().wait_recv()

        @pl.when(jnp.logical_not(at.has_up))
        def _():
            self.rise().wait_recv()

        out_ref[...] = self.sums[3]

        @pl.when(at.has_up)
        def _():
            out_ref[...] = out_ref[...] + self.came[3]
            self.rise().wait_send()

        @pl.when(at.has_down)
        def _():
            out_ref[...] = out_ref[...] + self.came[4]
            self.sink().wait_send()

        for kind in range(3):
            self.near(kind).wait_send()


def total_scratch(rows):
    return [
        pltpu.VMEM((6, rows, 128), F32),
        pltpu.VMEM((5, rows, 128), F32),
        pltpu.SemaphoreType.DMA((5,)),
        pltpu.SemaphoreType.DMA((5,)),
    ]


def scatter_scratch(levels):
    items = levels * CHUNKS
    h = CHUNK // 2
    return [
        pltpu.VMEM((levels, 2, 2, SHARD, D), BF16),
        pltpu.VMEM((2, 2, 2, CHUNK, D), BF16),
        pltpu.VMEM((items, 2, h, D), BF16),
        pltpu.VMEM((items, 2, CHUNK - h, D), BF16),
        pltpu.VMEM((items, CHUNK - h, D), BF16),
        pltpu.VMEM((items, h, D), BF16),
        pltpu.VMEM((items, CHUNK, D), BF16),
        pltpu.VMEM((items, CHUNK, D), BF16),
        pltpu.SemaphoreType.DMA((7, items)),
        pltpu.SemaphoreType.DMA((7, items)),
        pltpu.SemaphoreType.DMA((items,)),
    ]


def backward_head(
    pair,
    half,
    q_ref,
    k_ref,
    v_ref,
    bias_ref,
    g_ref,
    lt_ref,
    dt_ref,
    dq_ref,
    dk_ref,
    dv_ref,
    key_chunk,
):
    rows = q_ref.shape[0]
    keys = k_ref.shape[0]
    cols = pair_columns(pair)
    lane = lax.broadcasted_iota(jnp.int32, (key_chunk, LANES), 1)
    lane_q = lax.broadcasted_iota(jnp.int32, (rows, LANES), 1)
    own, own_q = lane // HEAD == half, lane_q // HEAD == half
    spare = lane == (1 - half) * HEAD
    query_pair = q_ref[:, cols]
    grad_pair = g_ref[:, cols]
    query = jnp.where(own_q, query_pair, jnp.ones_like(query_pair))
    mass = lt_ref[pl.ds(2 * pair + half, 1), :]
    inner = dt_ref[pl.ds(2 * pair + half, 1), :]
    zero = jnp.zeros((key_chunk, LANES), BF16)
    grad_query = jnp.zeros((rows, LANES), F32)
    for chunk in range(keys // key_chunk):
        part = pl.ds(chunk * key_chunk, key_chunk)
        key_pair = k_ref[part, cols]
        head_key = jnp.where(own, key_pair, jnp.where(spare, bias_ref[part, :], zero))
        head_value = jnp.where(own, v_ref[part, cols], zero)
        scores = back_product(head_key, query)
        soft = jnp.exp(scores - mass)
        grad_soft = back_product(head_value, grad_pair)
        grad_scores = (soft * (grad_soft - inner)).astype(BF16)
        grad_value = matmul(soft.astype(BF16), grad_pair).astype(BF16)
        grad_key = matmul(grad_scores, query_pair).astype(BF16)
        grad_query = grad_query + outer_sum(grad_scores, key_pair)
        dk_ref[part, cols] = jnp.where(own, grad_key, dk_ref[part, cols])
        dv_ref[part, cols] = jnp.where(own, grad_value, dv_ref[part, cols])
    merged = (grad_query * HEAD ** (-0.5)).astype(BF16)
    dq_ref[:, cols] = jnp.where(own_q, merged, dq_ref[:, cols])


def vector_row(vec_ref, first, count=D):
    low = first // 128
    return jnp.concatenate([vec_ref[low + i : low + i + 1, :] for i in range(count // 128)], axis=1)


def rows_of(ref, first, count):
    return ref[...].reshape(-1, D)[first : first + count]


ROW_CHUNK = 256


def forward_call_kernel(
    own_ref,
    vec_ref,
    in_ref,
    bias_ref,
    x_ref,
    n_ref,
    q_ref,
    k_ref,
    v_ref,
    o_ref,
    lt_ref,
    w0_ref,
    w1_ref,
    vecs_ref,
    l_ref,
    send0,
    recv0,
    send1,
    recv1,
    misc_send,
    misc_recv,
    local_sem,
    *vec_scratch,
):
    at = Place()
    rows = x_ref.shape[0]
    slots = rows // 2
    kept = pltpu.make_async_copy(in_ref.at[at.y], x_ref.at[pl.ds(0, slots)], local_sem.at[0])
    kept.start()

    def own_copy():
        first = pltpu.make_async_copy(own_ref, w0_ref.at[0, at.x, at.y, at.c], local_sem.at[1])
        later = pltpu.make_async_copy(
            own_ref, w1_ref.at[jnp.maximum(at.z - 1, 0), at.x, at.y, at.c], local_sem.at[1]
        )
        return first, later

    first_own, later_own = own_copy()

    @pl.when(at.z == 0)
    def _():
        first_own.start()

    @pl.when(at.z > 0)
    def _():
        later_own.start()

    sums, came, vec_send, vec_recv = vec_scratch
    sums[0] = vec_ref[...]
    total = Total(at, sums, came, vec_send, vec_recv)
    first_own.wait()
    at.barrier()

    swap = remote(
        in_ref.at[1 - at.y],
        x_ref.at[pl.ds(slots, slots)],
        misc_send.at[0],
        misc_recv.at[0],
        at.near_y,
    )
    base = Gather(at, w0_ref, send0, recv0, 0, 0, 0)
    rest = Gather(at, w1_ref, send1, recv1, 1, at.levels - 1, 48)

    total.step(0)
    swap.start()
    for number in range(3):
        base.step(number)
    kept.wait()

    def early(number, carry):
        base.step(number)
        total.step(number - 2)
        return carry

    lax.fori_loop(3, 10, early, 0)
    total.step(8)
    total.finish(vecs_ref)
    for number in range(3):
        rest.column(number)
    swap.wait_recv()
    gain = vector_row(vecs_ref, 0)
    shift = vector_row(vecs_ref, D)
    for chunk in range(rows // ROW_CHUNK):
        part = pl.ds(chunk * ROW_CHUNK, ROW_CHUNK)
        n_ref[part, :] = layer_norm(x_ref[part, :].astype(F32), gain, shift).astype(BF16)

    def late(number, carry):
        base.step(number)
        return carry

    lax.fori_loop(10, base.steps, late, 0)
    base.finish()

    bias_query = vector_row(vecs_ref, 2 * D)
    bias_value = vector_row(vecs_ref, 3 * D)
    w_key = rows_of(w0_ref, D, D)
    for chunk in range(rows // ROW_CHUNK):
        part = pl.ds(chunk * ROW_CHUNK, ROW_CHUNK)
        k_ref[part, :] = matmul(n_ref[part, :], w_key).astype(BF16)
    mine, other = pl.ds(0, rows), pl.ds(rows, rows)
    key_copy = remote(k_ref.at[mine], k_ref.at[other], misc_send.at[1], misc_recv.at[1], at.pair)
    value_copy = remote(v_ref.at[mine], v_ref.at[other], misc_send.at[2], misc_recv.at[2], at.pair)
    key_copy.start()
    w_value = rows_of(w0_ref, 2 * D, D)
    for chunk in range(rows // ROW_CHUNK):
        part = pl.ds(chunk * ROW_CHUNK, ROW_CHUNK)
        v_ref[part, :] = (matmul(n_ref[part, :], w_value) + bias_value).astype(BF16)
    value_copy.start()
    w_query = rows_of(w0_ref, 0, D)
    for chunk in range(rows // ROW_CHUNK):
        part = pl.ds(chunk * ROW_CHUNK, ROW_CHUNK)
        query = (matmul(n_ref[part, :], w_query) + bias_query).astype(BF16)
        q_ref[part, :] = query * jnp.asarray(HEAD ** (-0.5), BF16)
    rest.plane(0)
    l_ref[...] = jnp.zeros_like(l_ref)
    key_copy.wait_recv()
    value_copy.wait_recv()

    def pair_step(pair, carry):
        forward_pair(pair, q_ref, k_ref, v_ref, bias_ref, o_ref, l_ref, ROW_CHUNK)
        for extra in range(2):
            number = 2 * pair + extra + 1

            @pl.when(number > 2)
            def _(number=number):
                rest.column(number)

            rest.plane(number - 0)
            rest.diagonal(number - 1)
        return carry

    def rest_step(number, carry):
        rest.column(number)
        rest.plane(number)
        rest.diagonal(number - 1)
        return carry

    lax.fori_loop(0, PAIRS, pair_step, 0)
    lt_ref[...] = l_ref[...].T[: lt_ref.shape[0]]
    lax.fori_loop(2 * PAIRS + 1, rest.steps, rest_step, 0)
    rest.finish()
    swap.wait_send()
    key_copy.wait_send()
    value_copy.wait_send()


def forward_call(own, vec_part, inputs, bias, levels):
    rows = inputs.shape[0] * inputs.shape[1]
    vmem = pl.BlockSpec(memory_space=pltpu.VMEM)
    anywhere = pl.BlockSpec(memory_space=pl.ANY)
    slots = levels * CHUNKS
    low = lambda *shape: jax.ShapeDtypeStruct(shape, BF16)
    return pl.pallas_call(
        forward_call_kernel,
        out_shape=(
            low(rows, D),
            low(rows, D),
            low(rows, D),
            low(2 * rows, D),
            low(2 * rows, D),
            low(rows, D),
            jax.ShapeDtypeStruct((16, rows), F32),
            low(1, 2, 2, 2, SHARD, D),
            low(levels - 1, 2, 2, 2, SHARD, D),
            jax.ShapeDtypeStruct(vec_part.shape, F32),
        ),
        in_specs=[anywhere, vmem, anywhere, vmem],
        out_specs=(vmem,) * 8 + (anywhere, vmem),
        scratch_shapes=[
            pltpu.VMEM((rows, LANES), F32),
            pltpu.SemaphoreType.DMA((11, slots)),
            pltpu.SemaphoreType.DMA((11, slots)),
            pltpu.SemaphoreType.DMA((11, slots)),
            pltpu.SemaphoreType.DMA((11, slots)),
            pltpu.SemaphoreType.DMA((3,)),
            pltpu.SemaphoreType.DMA((3,)),
            pltpu.SemaphoreType.DMA((2,)),
        ]
        + total_scratch(vec_part.shape[0]),
        compiler_params=pltpu.CompilerParams(
            collective_id=0, has_side_effects=True, vmem_limit_bytes=VMEM_LIMIT
        ),
        name="gather_attend",
    )(own, vec_part, inputs, bias)


SCATTER_PARTS = 11


def backward_call_kernel(
    q_ref,
    k_ref,
    v_ref,
    bias_ref,
    g_ref,
    lt_ref,
    dt_ref,
    n_ref,
    x_ref,
    gm_ref,
    vecs_ref,
    vec_grad_ref,
    w0_ref,
    rest_ref,
    result_ref,
    outputs_ref,
    grad_in_ref,
    out_ref,
    vec_out_ref,
    dq_ref,
    dk_ref,
    dv_ref,
    rk_ref,
    rv_ref,
    gi_ref,
    g0_ref,
    pair_send,
    pair_recv,
    misc_send,
    misc_recv,
    misc_local,
    *scratch,
):
    at = Place()
    rows = x_ref.shape[0]
    slots = rows // 2
    mine, other = pl.ds(0, rows), pl.ds(rows, rows)
    kept, sent = pl.ds(0, slots), pl.ds(slots, slots)
    rest_scratch, scratch = scratch[:SCATTER_PARTS], scratch[SCATTER_PARTS:]
    base_scratch, scratch = scratch[:SCATTER_PARTS], scratch[SCATTER_PARTS:]
    sums, came, vec_send, vec_recv = scratch
    rest = Scatter(
        at, rest_ref, out_ref, rest_scratch[:8], *rest_scratch[8:], 1, at.levels - 1
    )
    base = Scatter(at, g0_ref, out_ref, base_scratch[:8], *base_scratch[8:], 0, 0)
    total = Total(at, sums, came, vec_send, vec_recv)
    out_kept = pltpu.make_async_copy(
        result_ref.at[kept], outputs_ref.at[at.y], misc_local.at[0]
    )
    out_kept.start()
    at.barrier()
    out_swap = remote(
        result_ref.at[sent], outputs_ref.at[at.y], misc_send.at[0], misc_recv.at[0], at.near_y
    )

    def exchange(kind, pair):
        source = (dk_ref, dv_ref)[kind]
        target = (rk_ref, rv_ref)[kind]
        return remote(
            source.at[other, pair_columns(pair)],
            target.at[:, pair_columns(pair)],
            pair_send.at[kind, pair],
            pair_recv.at[kind, pair],
            at.pair,
        )

    def head_step(head, carry):
        pair, half = head // 2, head % 2
        rest.step(head)
        backward_head(
            pair,
            half,
            q_ref,
            k_ref,
            v_ref,
            bias_ref,
            g_ref,
            lt_ref,
            dt_ref,
            dq_ref,
            dk_ref,
            dv_ref,
            ROW_CHUNK,
        )

        @pl.when(half == 1)
        def _():
            exchange(0, pair).start()
            exchange(1, pair).start()

        return carry

    lax.fori_loop(0, HEADS, head_step, 0)
    out_swap.start()
    rest.step(HEADS)

    def gather_pair(pair, carry):
        for kind in range(2):
            exchange(kind, pair).wait_recv()
        return carry

    lax.fori_loop(0, PAIRS, gather_pair, 0)
    for chunk in range(rows // ROW_CHUNK):
        part = pl.ds(chunk * ROW_CHUNK, ROW_CHUNK)
        dk_ref[part, :] = (dk_ref[part, :].astype(F32) + rk_ref[part, :].astype(F32)).astype(BF16)
        dv_ref[part, :] = (dv_ref[part, :].astype(F32) + rv_ref[part, :].astype(F32)).astype(BF16)
    grads = (dq_ref, dk_ref, dv_ref)
    for which in range(3):
        grad = grads[which][mine, :]
        for block in range(2):
            size = D // 2
            piece = outer_sum(n_ref[:, block * size : (block + 1) * size], grad).astype(BF16)
            for unit in range(size // CHUNK):
                number = (which * D + block * size) // CHUNK + unit
                shard = number // CHUNKS
                first = number % CHUNKS * CHUNK
                g0_ref[0, shard // 4, shard // 2 % 2, shard % 2, first : first + CHUNK, :] = piece[
                    unit * CHUNK : (unit + 1) * CHUNK
                ]
        if which < 2:
            rest.step(HEADS + 1 + which)
    base.step(0)
    for number in range(HEADS + 3, rest.steps):
        rest.step(number)
    base.step(1)
    sums[0] = vec_grad_ref[...]
    gain = vector_row(vecs_ref, 0)
    weights = [rows_of(w0_ref, which * D, D) for which in range(3)]
    column = [jnp.zeros((1, D), F32) for _ in range(4)]
    for chunk in range(rows // ROW_CHUNK):
        part = pl.ds(chunk * ROW_CHUNK, ROW_CHUNK)
        grad_normed = sum(back_product(grads[which][part, :], weights[which]) for which in range(3))
        frames = x_ref[part, :].astype(F32)
        centered = frames - jnp.mean(frames, axis=-1, keepdims=True)
        spread = lax.rsqrt(jnp.mean(centered * centered, axis=-1, keepdims=True) + 1e-05)
        unit_rows = centered * spread
        scaled = grad_normed * gain
        inner = jnp.mean(scaled * unit_rows, axis=-1, keepdims=True)
        shifted = scaled - jnp.mean(scaled, axis=-1, keepdims=True) - unit_rows * inner
        gi_ref[part, :] = (gm_ref[part, :] + spread * shifted).astype(BF16)
        parts = (
            grad_normed * unit_rows,
            grad_normed,
            dq_ref[part, :].astype(F32),
            dv_ref[part, :].astype(F32),
        )
        for i in range(4):
            column[i] = column[i] + jnp.sum(parts[i], axis=0, keepdims=True)
        base.step(2 + chunk)
    for i in range(4):
        for j in range(D // 128):
            sums[0, i * (D // 128) + j : i * (D // 128) + j + 1, :] = column[i][
                :, j * 128 : (j + 1) * 128
            ]
    total.step(0)
    in_kept = pltpu.make_async_copy(gi_ref.at[kept], grad_in_ref.at[at.y], misc_local.at[1])
    in_swap = remote(
        gi_ref.at[sent], grad_in_ref.at[at.y], misc_send.at[1], misc_recv.at[1], at.near_y
    )
    in_kept.start()
    in_swap.start()
    total.step(1)

    def last(number, carry):
        base.step(number)
        total.step(number - 3)
        return carry

    lax.fori_loop(2 + rows // ROW_CHUNK, total.steps + 3, last, 0)
    total.finish(vec_out_ref)
    base.finish()
    rest.finish()
    for swap in (out_swap, in_swap):
        swap.wait_send()
        swap.wait_recv()
    out_kept.wait()
    in_kept.wait()

    def sent_pair(pair, carry):
        for kind in range(2):
            exchange(kind, pair).wait_send()
        return carry

    lax.fori_loop(0, PAIRS, sent_pair, 0)


def backward_call(operands, rest, result, shape, levels):
    rows = shape[0] * shape[1]
    vec_rows = operands[11].shape[0]
    vmem = pl.BlockSpec(memory_space=pltpu.VMEM)
    anywhere = pl.BlockSpec(memory_space=pl.ANY)
    return pl.pallas_call(
        backward_call_kernel,
        out_shape=(
            jax.ShapeDtypeStruct(shape, BF16),
            jax.ShapeDtypeStruct(shape, BF16),
            jax.ShapeDtypeStruct((SHARD, D), F32),
            jax.ShapeDtypeStruct((vec_rows, 128), F32),
        ),
        in_specs=[vmem] * 13 + [anywhere] * 2,
        out_specs=(anywhere, anywhere, vmem, vmem),
        scratch_shapes=[
            pltpu.VMEM((rows, D), BF16),
            pltpu.VMEM((2 * rows, D), BF16),
            pltpu.VMEM((2 * rows, D), BF16),
            pltpu.VMEM((rows, D), BF16),
            pltpu.VMEM((rows, D), BF16),
            pltpu.VMEM((rows, D), BF16),
            pltpu.VMEM((1, 2, 2, 2, SHARD, D), BF16),
            pltpu.SemaphoreType.DMA((2, PAIRS)),
            pltpu.SemaphoreType.DMA((2, PAIRS)),
            pltpu.SemaphoreType.DMA((2,)),
            pltpu.SemaphoreType.DMA((2,)),
            pltpu.SemaphoreType.DMA((2,)),
        ]
        + scatter_scratch(levels - 1)
        + scatter_scratch(1)
        + total_scratch(vec_rows),
        compiler_params=pltpu.CompilerParams(
            collective_id=1, has_side_effects=True, vmem_limit_bytes=VMEM_LIMIT
        ),
        name="attend_scatter",
    )(*operands, rest, result)


def plain_local(inputs, lengths, matrices, vectors, cotangent):
    seq_count, local_slots, width = inputs.shape
    tok_size = lax.axis_size("tok")
    tok = lax.axis_index("tok")
    half = tok // 2
    devices = tok_size * lax.axis_size("seq")
    rows = seq_count * local_slots
    across = [(i, (i + 2) % 4) for i in range(4)]
    partner = [(i, i + 1 - 2 * (i % 2)) for i in range(4)]

    def pick(array, index):
        return lax.dynamic_index_in_dim(array, index, 0, keepdims=False)

    def to_sequence(array):
        other = lax.ppermute(pick(array, 1 - half), "tok", across)
        return jnp.concatenate([pick(array, half), other], axis=0)

    def from_sequence(array):
        other = lax.ppermute(array[local_slots:], "tok", across)
        kept = array[:local_slots]
        return jnp.where(half == 0, jnp.stack([kept, other]), jnp.stack([other, kept]))

    shard_rows = matrices.shape[0] // width
    low_rows = matrices.reshape(shard_rows, width).astype(BF16)
    gathered = lax.all_gather(low_rows, ("seq", "tok"), axis=0, tiled=True)
    w_query, w_key, w_value, w_out, w_up, w_down = split_matrices(gathered)
    vec_count = vectors.shape[0]
    vec_rows = 8
    vec_pad = vec_rows * 128 - vec_count
    vec_low = jnp.pad(vectors, (0, vec_pad)).astype(BF16).reshape(vec_rows, 128)
    vecs = lax.all_gather(vec_low, ("seq", "tok"), axis=0, tiled=True)
    vecs = vecs.reshape(devices, vec_rows * 128)[:, :vec_count].reshape(-1)
    (
        gain_one,
        first_norm_shift,
        bias_query,
        bias_value,
        bias_out,
        gain_two,
        shift_two,
        bias_up,
        bias_down,
    ) = split_vectors(vecs.astype(F32))

    token_rows = to_sequence(inputs).astype(F32)
    grad_out = to_sequence(cotangent)
    length = pick(lengths, half)
    slot = jnp.arange(local_slots, dtype=jnp.int32)
    places = jnp.concatenate([block * local_slots + slot for block in (tok, tok ^ 2, tok ^ 1, tok ^ 3)])
    bias = jnp.where(places < length, 0.0, -1e30).astype(BF16)[:, None]
    bias = jnp.broadcast_to(bias, (bias.shape[0], LANES))

    normed = layer_norm(token_rows, gain_one, first_norm_shift).astype(BF16)
    query = (matmul(normed, w_query) + bias_query).astype(BF16)
    scaled = query * jnp.asarray(HEAD ** (-0.5), BF16)
    keys_here = matmul(normed, w_key).astype(BF16)
    values_here = (matmul(normed, w_value) + bias_value).astype(BF16)
    keys = jnp.concatenate([keys_here, lax.ppermute(keys_here, "tok", partner)], axis=0)
    values = jnp.concatenate([values_here, lax.ppermute(values_here, "tok", partner)], axis=0)
    attended, lt = attend(scaled, keys, values, bias)
    middle = token_rows + (matmul(attended, w_out) + bias_out)
    normed_two = layer_norm(middle, gain_two, shift_two).astype(BF16)
    hidden = matmul(normed_two, w_up) + bias_up
    active = jax.nn.gelu(hidden, approximate=False).astype(BF16)
    result = middle + (matmul(active, w_down) + bias_down)
    outputs = from_sequence(result.astype(BF16))

    grad_out_wide = grad_out.astype(F32)
    d_down = outer_sum(active, grad_out)
    down_bias_gradient = column_sum(grad_out)
    grad_active = back_product(grad_out, w_down)
    gelu_value, gelu_pull = jax.vjp(partial(jax.nn.gelu, approximate=False), hidden)
    grad_hidden = gelu_pull(grad_active)[0].astype(BF16)
    d_up = outer_sum(normed_two, grad_hidden)
    d_bias_up = column_sum(grad_hidden)
    grad_normed_two = back_product(grad_hidden, w_up)
    norm_value, norm_pull = jax.vjp(layer_norm, middle, gain_two, shift_two)
    grad_mid_norm, d_gain_two, d_shift_two = norm_pull(grad_normed_two)
    grad_middle = grad_out_wide + grad_mid_norm
    grad_branch = grad_middle.astype(BF16)
    d_out = outer_sum(attended, grad_branch)
    d_bias_out = column_sum(grad_branch)
    grad_attended = back_product(grad_branch, w_out).astype(BF16)
    inner = (grad_attended.astype(F32) * attended.astype(F32)).reshape(rows, HEADS, HEAD).sum(-1)
    inner = jnp.pad(inner.T, ((0, 16 - HEADS), (0, 0)))
    grad_query, grad_keys, grad_values = attend_back(
        scaled, keys, values, bias, grad_attended, lt, inner
    )

    def pair_sum(array):
        other = lax.ppermute(array[rows:], "tok", partner)
        return (array[:rows].astype(F32) + other.astype(F32)).astype(BF16)

    grad_key = pair_sum(grad_keys)
    grad_value = pair_sum(grad_values)
    d_query = outer_sum(normed, grad_query)
    d_key = outer_sum(normed, grad_key)
    d_value = outer_sum(normed, grad_value)
    d_bias_query = column_sum(grad_query)
    d_bias_value = column_sum(grad_value)
    grad_normed = (
        back_product(grad_query, w_query)
        + back_product(grad_key, w_key)
        + back_product(grad_value, w_value)
    )
    first_value, leading_pullback = jax.vjp(layer_norm, token_rows, gain_one, first_norm_shift)
    grad_rows_norm, d_gain_one, d_shift_one = leading_pullback(grad_normed)
    grad_inputs = from_sequence((grad_middle + grad_rows_norm).astype(BF16))
    matrix_rows = jnp.concatenate(
        [
            piece.astype(BF16).reshape(-1, width)
            for piece in (d_query, d_key, d_value, d_out, d_up, d_down)
        ]
    )
    flat_vector_grads = jnp.concatenate(
        [
            d_gain_one,
            d_shift_one,
            d_bias_query,
            d_bias_value,
            d_bias_out,
            d_gain_two,
            d_shift_two,
            d_bias_up,
            down_bias_gradient,
        ]
    )
    vector_rows = jnp.pad(flat_vector_grads.reshape(devices, vec_count), ((0, 0), (0, vec_pad)))
    grad_rows = lax.psum_scatter(
        matrix_rows, ("seq", "tok"), scatter_dimension=0, tiled=True
    )
    grad_vec_rows = lax.psum_scatter(
        vector_rows.reshape(devices * vec_rows, 128), ("seq", "tok"), scatter_dimension=0, tiled=True
    )
    grad_matrices = grad_rows.astype(F32).reshape(-1)
    grad_vectors = grad_vec_rows.reshape(-1)[:vec_count]
    return (outputs, grad_inputs, grad_matrices, grad_vectors)


def fast_local(inputs, lengths, matrices, vectors, cotangent):
    seq_count, local_slots, width = inputs.shape
    tok = lax.axis_index("tok")
    half = tok // 2
    place = lax.axis_index("seq") * lax.axis_size("tok") + tok
    levels = lax.axis_size("seq") // 2
    devices = lax.axis_size("seq") * lax.axis_size("tok")
    rows = seq_count * local_slots
    across = [(i, (i + 2) % 4) for i in range(4)]

    def pick(array, index):
        return lax.dynamic_index_in_dim(array, index, 0, keepdims=False)

    def to_sequence(array):
        other = lax.ppermute(pick(array, 1 - half), "tok", across)
        return jnp.concatenate([pick(array, half), other], axis=0)

    own = matrices.reshape(SHARD, width).astype(BF16)
    vec_count = vectors.shape[0]
    vec_total = vec_count * devices
    vec_part = lax.dynamic_update_slice(
        jnp.zeros((vec_total,), F32), lax.reduce_precision(vectors, 8, 7), (place * vec_count,)
    ).reshape(vec_total // 128, 128)
    length = pick(lengths, half)
    slot = jnp.arange(local_slots, dtype=jnp.int32)
    places = jnp.concatenate(
        [block * local_slots + slot for block in (tok, tok ^ 2, tok ^ 1, tok ^ 3)]
    )
    bias = jnp.where(places < length, 0.0, -1e30).astype(BF16)[:, None]
    bias = jnp.broadcast_to(bias, (bias.shape[0], LANES))
    frames, normed, scaled, keys, values, attended, lt, w_first, w_rest, vecs = forward_call(
        own, vec_part, inputs, bias, levels
    )
    grad_out = to_sequence(cotangent)
    (
        gain_one,
        first_norm_shift,
        bias_query,
        bias_value,
        bias_out,
        gain_two,
        shift_two,
        bias_up,
        bias_down,
    ) = split_vectors(vecs.reshape(-1))
    rest_rows = w_rest.reshape(-1, width)
    w_out = rest_rows[:D]
    w_up = rest_rows[D : D + FF].reshape(D, FF)
    w_down = rest_rows[D + FF : D + 2 * FF]
    token_rows = frames.astype(F32)
    middle = token_rows + (matmul(attended, w_out) + bias_out)
    normed_two = layer_norm(middle, gain_two, shift_two).astype(BF16)
    hidden = matmul(normed_two, w_up) + bias_up
    active = jax.nn.gelu(hidden, approximate=False).astype(BF16)
    result = middle + (matmul(active, w_down) + bias_down)

    grad_out_wide = grad_out.astype(F32)
    d_down = outer_sum(active, grad_out)
    down_bias_gradient = column_sum(grad_out)
    grad_active = back_product(grad_out, w_down)
    gelu_value, gelu_pull = jax.vjp(partial(jax.nn.gelu, approximate=False), hidden)
    grad_hidden = gelu_pull(grad_active)[0].astype(BF16)
    d_up = outer_sum(normed_two, grad_hidden)
    d_bias_up = column_sum(grad_hidden)
    grad_normed_two = back_product(grad_hidden, w_up)
    norm_value, norm_pull = jax.vjp(layer_norm, middle, gain_two, shift_two)
    grad_mid_norm, d_gain_two, d_shift_two = norm_pull(grad_normed_two)
    grad_middle = grad_out_wide + grad_mid_norm
    grad_branch = grad_middle.astype(BF16)
    d_out = outer_sum(attended, grad_branch)
    d_bias_out = column_sum(grad_branch)
    grad_attended = back_product(grad_branch, w_out).astype(BF16)
    inner = (grad_attended.astype(F32) * attended.astype(F32)).reshape(rows, HEADS, HEAD).sum(-1)
    inner = jnp.pad(inner.T, ((0, 16 - HEADS), (0, 0)))
    nothing = jnp.zeros((D,), F32)
    vec_grads = jnp.concatenate(
        [nothing] * 4
        + [d_bias_out, d_gain_two, d_shift_two, d_bias_up, down_bias_gradient]
    ).reshape(vec_part.shape)
    rest_grads = jnp.concatenate(
        [piece.astype(BF16).reshape(-1, width) for piece in (d_out, d_up, d_down)]
    ).reshape(levels - 1, 2, 2, 2, SHARD, width)
    outputs, grad_inputs, grad_rows, grad_vecs = backward_call(
        (
            scaled,
            keys,
            values,
            bias,
            grad_attended,
            lt,
            inner,
            normed,
            frames,
            grad_middle,
            vecs,
            vec_grads,
            w_first,
        ),
        rest_grads,
        result.astype(BF16),
        inputs.shape,
        levels,
    )
    grad_matrices = grad_rows.reshape(-1)
    grad_vectors = lax.dynamic_slice(grad_vecs.reshape(-1), (place * vec_count,), (vec_count,))
    return (outputs, grad_inputs, grad_matrices, grad_vectors)


def solution(mesh):
    seq_size, tok_size = mesh.shape["seq"], mesh.shape["tok"]
    in_specs = (
        P("seq", "tok", None),
        P("seq"),
        P(("seq", "tok")),
        P(("seq", "tok")),
        P("seq", "tok", None),
    )
    out_specs = (P("seq", "tok", None), P("seq", "tok", None), P(("seq", "tok")), P(("seq", "tok")))
    whole_rows = (4 * D + 2 * FF) == seq_size * tok_size * SHARD
    body = fast_local if whole_rows and tok_size == 4 else plain_local
    return jax.shard_map(body, mesh=mesh, in_specs=in_specs, out_specs=out_specs, check_vma=False)
```
